256 devices in a mesh: dp: 16 (over y_hi, z), blk: 16 (over x, y_lo, core).
Axes of the slice: x: 4, y: 4 (y_hi: 2, y_lo: 2; y = y_hi * 2 + y_lo), z: 8, core: 2. Of those that a mesh axis runs over, the one named last changes fastest.
Arguments:
- visual_summary_vectors: bfloat16 [32768, 1792], P(('dp', 'blk')), may hold values from -24 to 24
- caption_summary_vectors: bfloat16 [32768, 1280], P(('dp', 'blk')), may hold values from -24 to 24
- pairing_identifiers: int32 [32768], P('dp'), may hold values from 0 to 1023
- valid_sample_tally: int32 [16, 16], P('dp'), may hold values from 64 to 128, as said below
- visual_mapping_matrix: bfloat16 [1792, 1536], replicated, may hold values from -0.125 to 0.125
- caption_mapping_matrix: bfloat16 [1280, 1536], replicated, may hold values from -0.15625 to 0.15625
- sharpness_factor: float32 [1], replicated, may hold values from 4 to 16
- score_shift_term: float32 [1], replicated, may hold values from -3 to -1
Outputs:
- per_sample_cost: float32 [32768], P(('dp', 'blk'))
- grad_image: float32 [1792, 1536], P('blk')
- grad_text: float32 [1280, 1536], P('blk')
The draws below stay inside these ranges and needn't reach their ends.
Inputs may be any that keep to these rules, and one draw needn't show every extreme that they name: `pairing_identifiers`: rows of one group with equal labels are positive pairs; a row's image and text share its label. `valid_sample_tally`: some device is full in every draw.
All inputs are finite; a program needn't handle non-finite values.
Results may differ from the reference program's by a relative error of at most 0.011.
Values may be sent and summed in bfloat16 or wider, within the bound.
A program may use at most 128 MiB of HBM per device.

```python
import math
import jax
import jax.numpy as jnp
from jax import lax

VIS_WIDTH = 1792
TXT_WIDTH = 1280
EMBED = 1536
ROWS = 128
BLOCKS = 16
GROUPS = 16
TOTAL = 32768


def draw_valid_sample_tally(key, part):
    values = jax.random.randint(key, (GROUPS, BLOCKS), ROWS // 2, ROWS + 1)
    chosen = jax.random.randint(jax.random.fold_in(key, 7), (), 0, GROUPS * BLOCKS)
    flattened = jnp.where(jnp.arange(GROUPS * BLOCKS) == chosen, ROWS, values.reshape(-1))
    return flattened.reshape(GROUPS, BLOCKS).astype(jnp.int32)


def with_ends(entries, rng, least, largest):
    extent = entries.shape
    spot = [jax.random.randint(jax.random.fold_in(rng, axis), (), 0, extent[axis]) for axis in range(len(extent))]
    entries = entries.at[tuple(spot)].set(least)
    longest = extent.index(max(extent))
    spot[longest] = (spot[longest] + 1) % extent[longest]
    return entries.at[tuple(spot)].set(largest)


def strengthened(drawn, own_key, source, target, shards_of, factor):
    def block_of(position):
        return (jnp.arange(drawn.shape[position]) // (drawn.shape[position] // shards_of)).reshape((-1,) + (1,) * (drawn.ndim - 1 - position))

    near = jax.random.permutation(own_key, shards_of)[block_of(target)]
    other_side = (block_of(target) + shards_of // 2) % shards_of
    return jnp.where((block_of(source) == near) | (block_of(source) == other_side), factor * drawn, drawn)


def block_scale(rng, dims, shards, smallest, largest):
    factor_of = 1.0
    for axis_at, parts in shards:
        heights = jax.random.uniform(jax.random.fold_in(jax.random.fold_in(rng, 6), axis_at), (parts,), jnp.float32, smallest / len(shards), largest / len(shards))
        factor_of = factor_of * jnp.repeat(jnp.exp(heights), dims[axis_at] // parts).reshape((-1,) + (1,) * (len(dims) - 1 - axis_at))
    return factor_of


def noise(stream_key, shape, spread, most, split=(), held_as=jnp.bfloat16):
    values = spread * jax.random.normal(stream_key, shape, jnp.float32)
    if split:
        values = values * block_scale(stream_key, shape, split, -0.22, 0.18)
    return jnp.clip(values, -most, most).astype(held_as)


def heavy_noise(own_key, shape, scale, most, cuts, heavy, kind=jnp.bfloat16):
    result = scale * jax.random.normal(own_key, shape, jnp.float32)
    if cuts:
        result = result * block_scale(own_key, shape, cuts, -0.22, 0.18)
    return jnp.clip(strengthened(result, jax.random.fold_in(own_key, 3), *heavy), -most, most).astype(kind)


def setup_inputs(seed: int = 0) -> dict:
    arg_keys = jax.random.split(jax.random.key(seed), 9)
    return {
        "visual_summary_vectors": heavy_noise(arg_keys[0], (TOTAL, VIS_WIDTH), 1.0, 24.0, ((0, 256),), (0, 1, 256, 6.0)),
        "caption_summary_vectors": heavy_noise(arg_keys[1], (TOTAL, TXT_WIDTH), 1.0, 24.0, ((0, 256),), (0, 1, 256, 6.0)),
        "pairing_identifiers": with_ends(jax.random.randint(arg_keys[2], (TOTAL,), 0, ROWS * BLOCKS // 2), jax.random.fold_in(arg_keys[2], 1), 0, (ROWS * BLOCKS // 2) - 1).astype(jnp.int32),
        "valid_sample_tally": draw_valid_sample_tally(jax.random.fold_in(arg_keys[8], 71), 0),
        "visual_mapping_matrix": noise(arg_keys[4], (VIS_WIDTH, EMBED), VIS_WIDTH ** -0.5, 0.125),
        "caption_mapping_matrix": noise(arg_keys[5], (TXT_WIDTH, EMBED), TXT_WIDTH ** -0.5, 0.15625),
        "sharpness_factor": jnp.clip(jnp.exp(jax.random.uniform(arg_keys[6], (1,), jnp.float32, math.log(4.0), math.log(16.0))), 4.0, 16.0),
        "score_shift_term": jnp.clip(jax.random.uniform(arg_keys[7], (1,), jnp.float32, -3.0, -1.0), -3.0, -1.0),
    }


loss_scale = 256.0
epsilon = 1e-06

def project(source, weights):
    projected = jnp.dot(source, weights, preferred_element_type=jnp.float32)
    length = jnp.sqrt(lax.optimization_barrier(jnp.sum(projected * projected, axis=1, keepdims=True)) + epsilon)
    return (projected / length, length)

def unit_backward(unit_rows, length, grad_unit):
    radial = lax.optimization_barrier(jnp.sum(unit_rows * grad_unit, axis=1, keepdims=True))
    return ((grad_unit - unit_rows * radial) / length).astype(jnp.bfloat16)

def round_trip(values):
    rounded = lax.optimization_barrier(values.astype(jnp.bfloat16))
    return rounded.astype(jnp.float32)

def cohort_sweep(cohort_operands, visual_mapping_matrix, caption_mapping_matrix, score_sharpness, additive_shift):
    visual_summary_vectors, caption_summary_vectors, pairing_identifiers, valid_sample_tally = cohort_operands
    group_rows = BLOCKS * ROWS
    unit_img, len_img = project(visual_summary_vectors, visual_mapping_matrix)
    unit_txt, len_txt = project(caption_summary_vectors, caption_mapping_matrix)
    visual_normalized_vector = unit_img.astype(jnp.bfloat16)
    caption_normalized_vector = unit_txt.astype(jnp.bfloat16)
    angular_similarity = jnp.dot(visual_normalized_vector, caption_normalized_vector.T, preferred_element_type=jnp.float32)
    similarity_scores = score_sharpness * angular_similarity + additive_shift
    positions = jnp.arange(group_rows)
    alive_rows = positions % ROWS < valid_sample_tally[positions // ROWS]
    weight = jnp.where(alive_rows[:, None] & alive_rows[None, :], 1.0, 0.0)
    target_sign = jnp.where(pairing_identifiers[:, None] == pairing_identifiers[None, :], 1.0, -1.0)
    per_sample_cost = lax.optimization_barrier(jnp.sum(jax.nn.softplus(-target_sign * similarity_scores) * weight, axis=1)) / group_rows
    sigmoid_derivatives = (-target_sign * jax.nn.sigmoid(-target_sign * similarity_scores) * weight * (loss_scale / group_rows)).astype(jnp.bfloat16)
    derivative_visual_unit = score_sharpness * jnp.dot(sigmoid_derivatives, caption_normalized_vector, preferred_element_type=jnp.float32)

    def add_partial(running, segment):
        derivative_fraction, visual_portion = segment
        interim_quantity = score_sharpness * jnp.dot(derivative_fraction.T, visual_portion, preferred_element_type=jnp.float32)
        return (running + round_trip(interim_quantity), None)
    grad_ztxt, _ = lax.scan(add_partial, jnp.zeros((group_rows, EMBED), jnp.float32), (sigmoid_derivatives.reshape(BLOCKS, ROWS, group_rows), visual_normalized_vector.reshape(BLOCKS, ROWS, EMBED)))
    return (per_sample_cost, unit_backward(unit_img, len_img, derivative_visual_unit), unit_backward(unit_txt, len_txt, grad_ztxt))

def reference(visual_summary_vectors, caption_summary_vectors, pairing_identifiers, valid_sample_tally, visual_mapping_matrix, caption_mapping_matrix, sharpness_factor, score_shift_term):
    score_sharpness = sharpness_factor[0]
    additive_shift = score_shift_term[0]
    group_rows = BLOCKS * ROWS
    cohort_operands = (visual_summary_vectors.reshape(GROUPS, group_rows, VIS_WIDTH), caption_summary_vectors.reshape(GROUPS, group_rows, TXT_WIDTH), pairing_identifiers.reshape(GROUPS, group_rows), valid_sample_tally)
    per_sample_cost, visual_change, caption_change = lax.map(lambda matrix_element: cohort_sweep(matrix_element, visual_mapping_matrix, caption_mapping_matrix, score_sharpness, additive_shift), cohort_operands)
    devices = GROUPS * BLOCKS

    def add_device(running, segment):
        visual_portion, text_part, image_grad, text_grad = segment
        first = running[0] + jnp.dot(visual_portion.T, image_grad, preferred_element_type=jnp.float32)
        second = running[1] + jnp.dot(text_part.T, text_grad, preferred_element_type=jnp.float32)
        return ((first, second), None)
    start_state = (jnp.zeros((VIS_WIDTH, EMBED), jnp.float32), jnp.zeros((TXT_WIDTH, EMBED), jnp.float32))
    (grad_image, grad_text), _ = lax.scan(add_device, start_state, (visual_summary_vectors.reshape(devices, ROWS, VIS_WIDTH), caption_summary_vectors.reshape(devices, ROWS, TXT_WIDTH), visual_change.reshape(devices, ROWS, EMBED), caption_change.reshape(devices, ROWS, EMBED)))
    return (per_sample_cost.reshape(-1), grad_image, grad_text)
```

```python
import functools

import jax
import jax.numpy as jnp
from jax import lax
from jax.experimental import pallas as pl
from jax.experimental.pallas import tpu as pltpu
from jax.sharding import PartitionSpec as P

loss_scale = 256.0
epsilon = 1e-06
MESH = pl.DeviceIdType.MESH
F32 = jnp.float32
BF16 = jnp.bfloat16


def kernel(
    total_rows, ring_z, labels, tally, sharp, shift, x_hbm, t_hbm, wv_hbm, wt_hbm,
    cost_out, gi_out, gt_out,
    wv, wt, xg, tg, zi, zt, inv_i, inv_t, u_scr, lab_i, row_rad, row_cost, txt_meta,
    slope, slope_t, stat_i, stat_t, sti_rcv, stt_rcv, stat_tot,
    gt_snd, gt_mrg, gt_rcv, gi_snd, gi_mrg, gi_rcv, d_img, d_txt, xg_t, tg_t,
    ei_snd, ei_mrg, ei_rcv, et_snd, et_mrg, et_rcv, tile, z_snd, z_rcv, y_snd, y_rcv, res, f_i, f_t,
    loc_sem, snd_sem, rcv_sem,
):
    rows = xg.shape[1]
    group = 4 * rows
    embed = zi.shape[1]
    width = embed // 4
    dp, blk = lax.axis_index("dp"), lax.axis_index("blk")
    x, q = lax.div(blk, 4), lax.rem(blk, 4)
    y, c = lax.div(q, 2), lax.rem(q, 2)
    z, yh = lax.rem(dp, ring_z), lax.div(dp, ring_z)
    xr, xl, xo = lax.rem(x + 1, 4), lax.rem(x + 3, 4), lax.rem(x + 2, 4)
    qp, qn, qd = y * 2 + 1 - c, (1 - y) * 2 + c, (1 - y) * 2 + 1 - c
    XR, XL, XO = (dp, xr * 4 + q), (dp, xl * 4 + q), (dp, xo * 4 + q)
    PT, YN, DG = (dp, x * 4 + qp), (dp, x * 4 + qn), (dp, x * 4 + qd)
    ZR = (yh * ring_z + lax.rem(z + 1, ring_z), blk)
    ZL = (yh * ring_z + lax.rem(z + ring_z - 1, ring_z), blk)
    YH = ((1 - yh) * ring_z + z, blk)

    barrier = pltpu.get_barrier_semaphore()
    peers = (XR, XL, XO, PT, YN, DG, ZR, ZL, YH)
    for peer in peers:
        pl.semaphore_signal(barrier, inc=1, device_id=peer, device_id_type=MESH)
    loc = [
        pltpu.make_async_copy(t_hbm, tg.at[x], loc_sem.at[0]),
        pltpu.make_async_copy(x_hbm, xg.at[q], loc_sem.at[1]),
        pltpu.make_async_copy(wt_hbm, wt, loc_sem.at[2]),
        pltpu.make_async_copy(wv_hbm, wv, loc_sem.at[3]),
    ]
    for copy in loc:
        copy.start()

    count = [0]
    started = []

    def slot():
        count[0] += 1
        return count[0] - 1

    def send(src, dst, sem, dev):
        copy = pltpu.make_async_remote_copy(
            src_ref=src, dst_ref=dst, send_sem=snd_sem.at[sem], recv_sem=rcv_sem.at[sem],
            device_id=dev, device_id_type=MESH,
        )
        copy.start()
        started.append(copy)

    def recv(dst, sem):
        pltpu.make_async_remote_copy(
            src_ref=dst, dst_ref=dst, send_sem=snd_sem.at[sem], recv_sem=rcv_sem.at[sem],
            device_id=XR, device_id_type=MESH,
        ).wait_recv()

    half = rows // 2
    halves = (pl.ds(0, half), pl.ds(half, half))

    pl.semaphore_wait(barrier, len(peers))
    loc[0].wait()
    t_sem = [slot() for _ in range(6)]
    send(tg.at[x, halves[0]], tg.at[x, halves[0]], t_sem[0], XR)
    send(tg.at[x, halves[1]], tg.at[x, halves[1]], t_sem[1], XL)
    send(tg.at[x, halves[1]], tg.at[x, halves[1]], t_sem[2], XR)
    send(tg.at[x, halves[0]], tg.at[x, halves[0]], t_sem[3], XL)
    loc[1].wait()
    x_sem = [slot() for _ in range(5)]
    for h in range(2):
        send(xg.at[q, halves[h]], xg.at[q, halves[h]], x_sem[h], YN)
    send(xg.at[q], xg.at[q], x_sem[2], PT)

    alive_lane = lax.broadcasted_iota(jnp.int32, (8, rows), 1)
    for k in range(4):
        cols = pl.ds(k * rows, rows)
        txt_meta[0:8, cols] = jnp.broadcast_to(labels[pl.ds(4 * k + q, 1), :], (8, rows)).astype(F32)
        txt_meta[8:16, cols] = jnp.where(alive_lane < tally[0, 4 * k + q], 1.0, 0.0)
        wide = jnp.broadcast_to(labels[pl.ds(4 * x + k, 1), :].astype(F32), (rows, rows))
        lab_i[pl.ds(k * rows, rows), :] = wide.T

    def project(source, weights, unit, inverse, k):
        def body(j, carry):
            cols = pl.ds(pl.multiple_of(j * 512, 512), 512)
            u_scr[:, cols] = jnp.dot(source[k], weights[:, cols], preferred_element_type=F32)
            return carry

        lax.fori_loop(0, embed // 512, body, 0)
        u = u_scr[...]
        inv = 1.0 / jnp.sqrt(jnp.sum(u * u, axis=1, keepdims=True) + epsilon)
        at = pl.ds(pl.multiple_of(k * rows, rows), rows)
        unit[at, :] = (u * inv).astype(BF16)
        inverse[at, :] = jnp.broadcast_to(inv, (rows, rows))

    loc[2].wait()
    project(tg, wt, zt, inv_t, x)
    recv(tg.at[xl, halves[0]], t_sem[0])
    send(tg.at[xl, halves[0]], tg.at[xl, halves[0]], t_sem[4], XR)
    recv(tg.at[xr, halves[1]], t_sem[1])
    send(tg.at[xr, halves[1]], tg.at[xr, halves[1]], t_sem[5], XL)
    loc[3].wait()
    project(xg, wv, zi, inv_i, q)
    recv(xg.at[qp], x_sem[2])
    recv(xg.at[qn, halves[0]], x_sem[0])
    send(xg.at[qn, halves[0]], xg.at[qn, halves[0]], x_sem[3], PT)
    project(xg, wv, zi, inv_i, qp)
    recv(tg.at[xl, halves[1]], t_sem[2])
    project(tg, wt, zt, inv_t, xl)
    recv(xg.at[qn, halves[1]], x_sem[1])
    send(xg.at[qn, halves[1]], xg.at[qn, halves[1]], x_sem[4], PT)
    recv(tg.at[xr, halves[0]], t_sem[3])
    project(tg, wt, zt, inv_t, xr)
    project(xg, wv, zi, inv_i, qn)
    recv(tg.at[xo, halves[0]], t_sem[4])
    recv(tg.at[xo, halves[1]], t_sem[5])
    project(tg, wt, zt, inv_t, xo)
    recv(xg.at[qd, halves[0]], x_sem[3])
    recv(xg.at[qd, halves[1]], x_sem[4])
    project(xg, wv, zi, inv_i, qd)

    scale = sharp[0]
    bias = shift[0]
    stat_t[...] = jnp.zeros_like(stat_t)

    def pair_block(k, carry):
        at = pl.ds(pl.multiple_of(k * rows, rows), rows)
        cosine = lax.dot_general(
            zi[at, :], zt[...], (((1,), (1,)), ((), ())), preferred_element_type=F32
        )
        same = lab_i[at, 0:1] == txt_meta[0:1, :]
        limit = tally[0, 4 * x + k]
        alive = lax.broadcasted_iota(jnp.int32, (rows, 1), 0) < limit
        weight = jnp.where(alive, 1.0, 0.0) * txt_meta[8:9, :]
        sign = jnp.where(same, 1.0, -1.0)
        t = -sign * (scale * cosine + bias)
        e = jnp.exp(-jnp.abs(t))
        cost = (jnp.maximum(t, 0.0) + jnp.log1p(e)) * weight
        sigmoid = jnp.where(t >= 0.0, 1.0, e) / (1.0 + e)
        s = -sign * sigmoid * weight * (loss_scale / total_rows)
        s16 = s.astype(BF16)
        slope[at, :] = s16
        s = s16.astype(F32)
        slope_t[:, at] = s.T.astype(BF16)
        along = s * cosine * scale
        row_rad[at, :] = jnp.broadcast_to(jnp.sum(along, axis=1, keepdims=True), (rows, rows))
        row_cost[at, :] = jnp.broadcast_to(jnp.sum(cost, axis=1, keepdims=True), (rows, rows))
        stat_t[...] += jnp.broadcast_to(jnp.sum(along, axis=0, keepdims=True), stat_t.shape)
        return carry

    lax.fori_loop(0, 4, pair_block, 0)
    stat_i[0:8, :] = row_rad[...].T[0:8, :]
    stat_i[8:16, :] = row_cost[...].T[0:8, :]

    def width_at(k):
        return pl.ds(pl.multiple_of(k * width, 128), width)

    def txt_part(k):
        gt_snd[k] = (
            scale * jnp.dot(slope_t[...], zi[:, width_at(k)], preferred_element_type=F32)
        ).astype(BF16)

    def img_part(k):
        gi_snd[k] = (
            scale * jnp.dot(slope[...], zt[:, width_at(k)], preferred_element_type=F32)
        ).astype(BF16)

    class RingSum:
        def __init__(self, snd, mrg, rcv):
            self.snd, self.mrg, self.rcv = snd, mrg, rcv
            h = snd.shape[1] // 2
            self.h, self.a, self.b = h, pl.ds(0, h), pl.ds(h, h)
            self.sems = [slot() for _ in range(6)]

        def far(self):
            send(self.snd.at[xo, self.a], self.rcv.at[0], self.sems[0], XR)
            send(self.snd.at[xo, self.b], self.rcv.at[1], self.sems[1], XL)

        def near(self):
            send(self.snd.at[xr, self.b], self.rcv.at[4], self.sems[4], XR)
            send(self.snd.at[xl, self.a], self.rcv.at[5], self.sems[5], XL)

        def merge(self):
            recv(self.rcv.at[0], self.sems[0])
            self.mrg[0] = (self.rcv[0].astype(F32) + self.snd[xr, self.a].astype(F32)).astype(BF16)
            send(self.mrg.at[0], self.rcv.at[2], self.sems[2], XR)
            recv(self.rcv.at[1], self.sems[1])
            self.mrg[1] = (self.rcv[1].astype(F32) + self.snd[xl, self.b].astype(F32)).astype(BF16)
            send(self.mrg.at[1], self.rcv.at[3], self.sems[3], XL)

        def arrive(self):
            for i in (4, 5, 2, 3):
                recv(self.rcv.at[i], self.sems[i])

        def top(self, start, size):
            at = pl.ds(start, size)
            return self.snd[x, at].astype(F32) + self.rcv[2, at].astype(F32) + self.rcv[5, at].astype(F32)

        def low(self, start, size):
            at = pl.ds(start, size)
            mine = self.snd[x, pl.ds(self.h + start, size)].astype(F32)
            return mine + self.rcv[3, at].astype(F32) + self.rcv[4, at].astype(F32)

    class PairSum:
        def __init__(self, snd, mrg, rcv):
            self.snd, self.mrg, self.rcv = snd, mrg, rcv
            self.sems = [slot() for _ in range(3)]

        def far(self):
            send(self.snd.at[qd], self.rcv.at[0], self.sems[0], PT)

        def near(self):
            send(self.snd.at[qp], self.rcv.at[1], self.sems[1], PT)

        def merge(self):
            recv(self.rcv.at[0], self.sems[0])
            self.mrg[...] = (self.rcv[0].astype(F32) + self.snd[qn].astype(F32)).astype(BF16)
            send(self.mrg, self.rcv.at[2], self.sems[2], YN)

        def arrive(self):
            recv(self.rcv.at[1], self.sems[1])
            recv(self.rcv.at[2], self.sems[2])

        def total(self, start, size):
            at = pl.ds(start, size)
            return self.snd[q, at].astype(F32) + self.rcv[1, at].astype(F32) + self.rcv[2, at].astype(F32)

    st_sem = [slot() for _ in range(6)]
    for i, dev in enumerate((XR, XL, XO)):
        send(stat_t, stt_rcv.at[i], st_sem[i], dev)
    for i, dev in enumerate((PT, YN, DG)):
        send(stat_i, sti_rcv.at[i], st_sem[3 + i], dev)

    txt_sum = RingSum(gt_snd, gt_mrg, gt_rcv)
    img_sum = PairSum(gi_snd, gi_mrg, gi_rcv)
    txt_part(xo)
    txt_sum.far()
    img_part(qd)
    img_sum.far()
    txt_part(xr)
    txt_part(xl)
    txt_sum.near()
    img_part(qn)
    img_sum.merge()
    img_part(qp)
    img_sum.near()
    img_part(q)
    txt_part(x)
    txt_sum.merge()
    for k in range(4):
        xg_t[:, k * rows : (k + 1) * rows] = xg[k].T

    for i in range(3):
        recv(sti_rcv.at[i], st_sem[3 + i])
    stat_tot[...] = stat_i[...] + sti_rcv[0] + sti_rcv[1] + sti_rcv[2]
    row_rad[...] = jnp.broadcast_to(stat_tot[0:1, :], (rows, group)).T
    cost_out[...] = stat_tot[8:9, pl.ds(pl.multiple_of(q * rows, rows), rows)] * (1.0 / total_rows)

    def change(out, unit, inverse, k, column, total):
        at = pl.ds(k * rows, rows)
        u = unit[at, width_at(column)].astype(F32)
        out[at, :] = ((total - u * row_rad[at, 0:1]) * inverse[at, 0:1]).astype(BF16)

    img_sum.arrive()
    for k in range(4):
        change(d_img, zi, inv_i, k, q, img_sum.total(k * rows, rows))

    part_i = RingSum(ei_snd, ei_mrg, ei_rcv)
    deep = ei_snd.shape[1]

    def image_rows(k):
        at = pl.ds(pl.multiple_of(k * deep, 64), deep)
        ei_snd[k] = jnp.dot(xg_t[at, :], d_img[...], preferred_element_type=F32).astype(BF16)

    image_rows(xo)
    part_i.far()
    image_rows(xr)
    image_rows(xl)
    part_i.near()

    for k in range(4):
        tg_t[:, k * rows : (k + 1) * rows] = tg[k].T
    for i in range(3):
        recv(stt_rcv.at[i], st_sem[i])
    txt_total = stat_t[0:1, :] + stt_rcv[0, 0:1, :] + stt_rcv[1, 0:1, :] + stt_rcv[2, 0:1, :]
    row_rad[...] = jnp.broadcast_to(txt_total, (rows, group)).T
    txt_sum.arrive()
    for k in range(2):
        change(d_txt, zt, inv_t, k, x, txt_sum.top(k * rows, rows))
    for k in range(2):
        change(d_txt, zt, inv_t, 2 + k, x, txt_sum.low(k * rows, rows))

    part_t = PairSum(et_snd, et_mrg, et_rcv)
    own_t = gt_out.shape[0]
    own_i = gi_out.shape[0]
    for k in range(4):
        part = jnp.dot(
            tg_t[4 * own_t * k : 4 * own_t * (k + 1), :], d_txt[...], preferred_element_type=F32
        ).astype(BF16)
        for owner in range(4):
            et_snd[owner, own_t * k : own_t * (k + 1), :] = part[own_t * owner : own_t * (owner + 1)]
    part_t.far()
    part_t.near()
    part_i.merge()
    image_rows(x)
    part_t.merge()

    part_i.arrive()
    tile[0 : deep // 2, :] = part_i.top(0, deep // 2)
    tile[deep // 2 : deep, :] = part_i.low(0, deep // 2)
    part_t.arrive()
    tile[deep : deep + 4 * own_t, :] = part_t.total(0, 4 * own_t)

    piece = y_snd.shape[0]
    plus, minus = ring_z // 2, (ring_z - 1) // 2

    def piece_at(k):
        return pl.ds(pl.multiple_of(lax.rem(k + ring_z, ring_z) * piece, 16), piece)

    p_sem = [slot() for _ in range(plus)]
    m_sem = [slot() for _ in range(minus)]
    for s in range(plus):
        value = tile[piece_at(z + plus - s), :]
        if s:
            recv(z_rcv.at[s - 1], p_sem[s - 1])
            value = value + z_rcv[s - 1].astype(F32)
        z_snd[s] = value.astype(BF16)
        send(z_snd.at[s], z_rcv.at[s], p_sem[s], ZR)
        if s < minus:
            value = tile[piece_at(z - (minus - s)), :]
            if s:
                recv(z_rcv.at[plus + s - 1], m_sem[s - 1])
                value = value + z_rcv[plus + s - 1].astype(F32)
            z_snd[plus + s] = value.astype(BF16)
            send(z_snd.at[plus + s], z_rcv.at[plus + s], m_sem[s], ZL)
    recv(z_rcv.at[plus + minus - 1], m_sem[minus - 1])
    recv(z_rcv.at[plus - 1], p_sem[plus - 1])
    value = tile[piece_at(z), :] + z_rcv[plus - 1].astype(F32) + z_rcv[plus + minus - 1].astype(F32)
    y_snd[...] = value.astype(BF16)
    y_sem = slot()
    send(y_snd, y_rcv, y_sem, YH)
    recv(y_rcv, y_sem)
    res[piece_at(z), :] = (y_snd[...].astype(F32) + y_rcv[...].astype(F32)).astype(BF16)
    p_sem = [slot() for _ in range(plus)]
    m_sem = [slot() for _ in range(minus)]
    for s in range(plus):
        if s:
            recv(res.at[piece_at(z - s)], p_sem[s - 1])
        send(res.at[piece_at(z - s)], res.at[piece_at(z - s)], p_sem[s], ZR)
        if s < minus:
            if s:
                recv(res.at[piece_at(z + s)], m_sem[s - 1])
            send(res.at[piece_at(z + s)], res.at[piece_at(z + s)], m_sem[s], ZL)
    recv(res.at[piece_at(z + minus)], m_sem[minus - 1])
    recv(res.at[piece_at(z - plus)], p_sem[plus - 1])

    def image_owner(k):
        return pl.ds(pl.multiple_of(k * own_i, 16), own_i)

    def text_owner(k):
        return pl.ds(pl.multiple_of(deep + k * own_t, 16), own_t)

    o_sem = [slot() for _ in range(6)]
    for i, (k, dev) in enumerate(((qd, DG), (qn, YN), (qp, PT))):
        send(res.at[image_owner(k)], f_i.at[q], o_sem[i], dev)
    for i, (k, dev) in enumerate(((xo, XO), (xr, XR), (xl, XL))):
        send(res.at[text_owner(k)], f_t.at[x], o_sem[3 + i], dev)
    gi_out[:, width_at(q)] = res[image_owner(q), :].astype(F32)
    gt_out[:, width_at(x)] = res[text_owner(x), :].astype(F32)
    for i, k in ((2, qp), (1, qn), (0, qd)):
        recv(f_i.at[k], o_sem[i])
        gi_out[:, width_at(k)] = f_i[k].astype(F32)
    for i, k in ((4, xl), (5, xr), (3, xo)):
        recv(f_t.at[k], o_sem[i])
        gt_out[:, width_at(k)] = f_t[k].astype(F32)

    for copy in started:
        copy.wait_send()


def solution(mesh):
    blocks = mesh.shape["blk"]
    ring_z = mesh.shape["dp"] // 2

    def on_device(
        visual_summary_vectors, caption_summary_vectors, pairing_identifiers, valid_sample_tally,
        visual_mapping_matrix, caption_mapping_matrix, sharpness_factor, score_shift_term,
    ):
        rows, deep_i = visual_summary_vectors.shape
        deep_t, embed = caption_mapping_matrix.shape
        group, width = 4 * rows, embed // 4
        own_i, own_t = deep_i // blocks, deep_t // blocks
        area = 4 * (own_i + own_t)
        piece = area // ring_z
        vmem = pl.BlockSpec(memory_space=pltpu.VMEM)
        smem = pl.BlockSpec(memory_space=pltpu.SMEM)
        hbm = pl.BlockSpec(memory_space=pl.ANY)
        B = lambda *shape: pltpu.VMEM(shape, BF16)
        F = lambda *shape: pltpu.VMEM(shape, F32)
        cost, grad_image, grad_text = pl.pallas_call(
            functools.partial(kernel, blocks * rows, ring_z),
            out_shape=(
                jax.ShapeDtypeStruct((1, rows), F32),
                jax.ShapeDtypeStruct((own_i, embed), F32),
                jax.ShapeDtypeStruct((own_t, embed), F32),
            ),
            in_specs=[vmem, smem, smem, smem, hbm, hbm, hbm, hbm],
            out_specs=(vmem, vmem, vmem),
            scratch_shapes=[
                B(deep_i, embed), B(deep_t, embed), B(4, rows, deep_i), B(4, rows, deep_t),
                B(group, embed), B(group, embed), F(group, rows), F(group, rows), F(rows, embed),
                F(group, rows), F(group, rows), F(group, rows), F(16, group),
                B(group, group), B(group, group), F(16, group), F(8, group),
                F(3, 16, group), F(3, 8, group), F(16, group),
                B(4, group, width), B(2, group // 2, width), B(6, group // 2, width),
                B(4, group, width), B(group, width), B(3, group, width),
                B(group, width), B(group, width), B(deep_i, group), B(deep_t, group),
                B(4, 4 * own_i, width), B(2, 2 * own_i, width), B(6, 2 * own_i, width),
                B(4, 4 * own_t, width), B(4 * own_t, width), B(3, 4 * own_t, width),
                F(area, width), B(ring_z - 1, piece, width), B(ring_z - 1, piece, width),
                B(piece, width), B(piece, width), B(area, width),
                B(4, own_i, width), B(4, own_t, width),
                pltpu.SemaphoreType.DMA((4,)),
                pltpu.SemaphoreType.DMA((64,)),
                pltpu.SemaphoreType.DMA((64,)),
            ],
            compiler_params=pltpu.CompilerParams(
                collective_id=0, has_side_effects=True, vmem_limit_bytes=60 * 1024 * 1024
            ),
            name="contrastive_step",
        )(
            pairing_identifiers.reshape(blocks, rows), valid_sample_tally, sharpness_factor, score_shift_term,
            visual_summary_vectors, caption_summary_vectors, visual_mapping_matrix, caption_mapping_matrix,
        )
        return cost.reshape(rows), grad_image, grad_text

    placed = (
        P(("dp", "blk"), None), P(("dp", "blk"), None), P("dp"), P("dp", None), P(), P(), P(), P(),
    )
    return jax.shard_map(
        on_device,
        mesh=mesh,
        in_specs=placed,
        out_specs=(P(("dp", "blk")), P("blk", None), P("blk", None)),
        check_vma=False,
    )
```

```python
import functools

import jax
import jax.numpy as jnp
from jax import lax
from jax.experimental import pallas as pl
from jax.experimental.pallas import tpu as pltpu
from jax.sharding import PartitionSpec as P

loss_scale = 256.0
epsilon = 1e-06
MESH = pl.DeviceIdType.MESH
F32 = jnp.float32
BF16 = jnp.bfloat16
ORDER = (0, "t", 2, 0, 2, "i", 1) + (0, 2, 1) * 7 + (0, 2, 1, 1)


def kernel(
    total_rows, ring_z, lab_hbm, tal_hbm, sha_hbm, shi_hbm, x_hbm, t_hbm, wv_hbm, wt_hbm,
    cost_out, f_i, f_t,
    labels, tally, sharp, shift,
    wv, wt, xg, tg, zi, zt, inv_i, inv_t, u_scr, lab_i, row_rad, row_cost, txt_meta,
    slope, slope_t, stat_i, stat_t, sti_rcv, stt_rcv, stat_tot,
    gt_snd, gt_mrg, gt_rcv, gi_snd, gi_mrg, gi_rcv, d_img, d_txt, xg_t, tg_t,
    e0_snd, e0_mrg, e0_rcv, e1_snd, e1_mrg, e1_rcv, et_snd, et_mrg, et_rcv, tile, z_snd, z_rcv, y_snd, y_rcv, res,
    loc_sem, snd_sem, rcv_sem,
):
    rows = xg.shape[1]
    group = 4 * rows
    embed = zi.shape[1]
    width = embed // 4
    dp, blk = lax.axis_index("dp"), lax.axis_index("blk")
    x, q = lax.div(blk, 4), lax.rem(blk, 4)
    y, c = lax.div(q, 2), lax.rem(q, 2)
    z, yh = lax.rem(dp, ring_z), lax.div(dp, ring_z)
    xr, xl, xo = lax.rem(x + 1, 4), lax.rem(x + 3, 4), lax.rem(x + 2, 4)
    qp, qn, qd = y * 2 + 1 - c, (1 - y) * 2 + c, (1 - y) * 2 + 1 - c
    XR, XL, XO = (dp, xr * 4 + q), (dp, xl * 4 + q), (dp, xo * 4 + q)
    PT, YN, DG = (dp, x * 4 + qp), (dp, x * 4 + qn), (dp, x * 4 + qd)
    ZR = (yh * ring_z + lax.rem(z + 1, ring_z), blk)
    ZL = (yh * ring_z + lax.rem(z + ring_z - 1, ring_z), blk)
    YH = ((1 - yh) * ring_z + z, blk)

    barrier = pltpu.get_barrier_semaphore()
    peers = (XR, XL, XO, PT, YN, DG, ZR, ZL, YH)
    for peer in peers:
        pl.semaphore_signal(barrier, inc=1, device_id=peer, device_id_type=MESH)
    loc = [
        pltpu.make_async_copy(t_hbm, tg.at[x], loc_sem.at[0]),
        pltpu.make_async_copy(x_hbm, xg.at[q], loc_sem.at[1]),
        pltpu.make_async_copy(wt_hbm, wt, loc_sem.at[2]),
        pltpu.make_async_copy(wv_hbm, wv, loc_sem.at[3]),
        pltpu.make_async_copy(lab_hbm, labels, loc_sem.at[4]),
        pltpu.make_async_copy(tal_hbm, tally, loc_sem.at[5]),
        pltpu.make_async_copy(sha_hbm, sharp, loc_sem.at[6]),
        pltpu.make_async_copy(shi_hbm, shift, loc_sem.at[7]),
    ]
    for copy in loc:
        copy.start()

    count = [0]
    started = []

    def slot():
        count[0] += 1
        return count[0] - 1

    def send(src, dst, sem, dev):
        copy = pltpu.make_async_remote_copy(
            src_ref=src, dst_ref=dst, send_sem=snd_sem.at[sem], recv_sem=rcv_sem.at[sem],
            device_id=dev, device_id_type=MESH,
        )
        copy.start()
        started.append(copy)

    def recv(dst, sem):
        pltpu.make_async_remote_copy(
            src_ref=dst, dst_ref=dst, send_sem=snd_sem.at[sem], recv_sem=rcv_sem.at[sem],
            device_id=XR, device_id_type=MESH,
        ).wait_recv()

    half = rows // 2
    halves = (pl.ds(0, half), pl.ds(half, half))

    pl.semaphore_wait(barrier, len(peers))
    loc[0].wait()
    t_sem = [slot() for _ in range(6)]
    send(tg.at[x, halves[0]], tg.at[x, halves[0]], t_sem[0], XR)
    send(tg.at[x, halves[1]], tg.at[x, halves[1]], t_sem[1], XL)
    send(tg.at[x, halves[1]], tg.at[x, halves[1]], t_sem[2], XR)
    send(tg.at[x, halves[0]], tg.at[x, halves[0]], t_sem[3], XL)
    loc[1].wait()
    x_sem = [slot() for _ in range(5)]
    for h in range(2):
        send(xg.at[q, halves[h]], xg.at[q, halves[h]], x_sem[h], YN)
    send(xg.at[q], xg.at[q], x_sem[2], PT)

    for copy in loc[4:]:
        copy.wait()
    alive_lane = lax.broadcasted_iota(jnp.int32, (8, rows), 1)
    for k in range(4):
        cols = pl.ds(k * rows, rows)
        txt_meta[0:8, cols] = jnp.broadcast_to(labels[pl.ds(4 * k + q, 1), :], (8, rows)).astype(F32)
        txt_meta[8:16, cols] = jnp.where(alive_lane < tally[0, 4 * k + q], 1.0, 0.0)
        wide = jnp.broadcast_to(labels[pl.ds(4 * x + k, 1), :].astype(F32), (rows, rows))
        lab_i[pl.ds(k * rows, rows), :] = wide.T

    def project(source, weights, unit, inverse, k):
        def body(j, carry):
            cols = pl.ds(pl.multiple_of(j * 512, 512), 512)
            u_scr[:, cols] = jnp.dot(source[k], weights[:, cols], preferred_element_type=F32)
            return carry

        lax.fori_loop(0, embed // 512, body, 0)
        u = u_scr[...]
        inv = 1.0 / jnp.sqrt(jnp.sum(u * u, axis=1, keepdims=True) + epsilon)
        at = pl.ds(pl.multiple_of(k * rows, rows), rows)
        unit[at, :] = (u * inv).astype(BF16)
        inverse[at, :] = jnp.broadcast_to(inv, (rows, rows))

    loc[2].wait()
    project(tg, wt, zt, inv_t, x)
    recv(tg.at[xl, halves[0]], t_sem[0])
    send(tg.at[xl, halves[0]], tg.at[xl, halves[0]], t_sem[4], XR)
    recv(tg.at[xr, halves[1]], t_sem[1])
    send(tg.at[xr, halves[1]], tg.at[xr, halves[1]], t_sem[5], XL)
    loc[3].wait()
    project(xg, wv, zi, inv_i, q)
    recv(xg.at[qp], x_sem[2])
    recv(xg.at[qn, halves[0]], x_sem[0])
    send(xg.at[qn, halves[0]], xg.at[qn, halves[0]], x_sem[3], PT)
    project(xg, wv, zi, inv_i, qp)
    recv(tg.at[xl, halves[1]], t_sem[2])
    project(tg, wt, zt, inv_t, xl)
    recv(xg.at[qn, halves[1]], x_sem[1])
    send(xg.at[qn, halves[1]], xg.at[qn, halves[1]], x_sem[4], PT)
    recv(tg.at[xr, halves[0]], t_sem[3])
    project(tg, wt, zt, inv_t, xr)
    project(xg, wv, zi, inv_i, qn)
    recv(tg.at[xo, halves[0]], t_sem[4])
    recv(tg.at[xo, halves[1]], t_sem[5])
    project(tg, wt, zt, inv_t, xo)
    recv(xg.at[qd, halves[0]], x_sem[3])
    recv(xg.at[qd, halves[1]], x_sem[4])
    project(xg, wv, zi, inv_i, qd)

    scale = sharp[0]
    bias = shift[0]
    stat_t[...] = jnp.zeros_like(stat_t)

    def pair_block(k, carry):
        at = pl.ds(pl.multiple_of(k * rows, rows), rows)
        cosine = lax.dot_general(
            zi[at, :], zt[...], (((1,), (1,)), ((), ())), preferred_element_type=F32
        )
        same = lab_i[at, 0:1] == txt_meta[0:1, :]
        limit = tally[0, 4 * x + k]
        alive = lax.broadcasted_iota(jnp.int32, (rows, 1), 0) < limit
        weight = jnp.where(alive, 1.0, 0.0) * txt_meta[8:9, :]
        sign = jnp.where(same, 1.0, -1.0)
        t = -sign * (scale * cosine + bias)
        e = jnp.exp(-jnp.abs(t))
        cost = (jnp.maximum(t, 0.0) + jnp.log1p(e)) * weight
        sigmoid = jnp.where(t >= 0.0, 1.0, e) / (1.0 + e)
        s = -sign * sigmoid * weight * (loss_scale / total_rows)
        s16 = s.astype(BF16)
        slope[at, :] = s16
        s = s16.astype(F32)
        slope_t[:, at] = s.T.astype(BF16)
        along = s * cosine * scale
        row_rad[at, :] = jnp.broadcast_to(jnp.sum(along, axis=1, keepdims=True), (rows, rows))
        row_cost[at, :] = jnp.broadcast_to(jnp.sum(cost, axis=1, keepdims=True), (rows, rows))
        stat_t[...] += jnp.broadcast_to(jnp.sum(along, axis=0, keepdims=True), stat_t.shape)
        return carry

    lax.fori_loop(0, 4, pair_block, 0)
    stat_i[0:8, :] = row_rad[...].T[0:8, :]
    stat_i[8:16, :] = row_cost[...].T[0:8, :]

    def width_at(k):
        return pl.ds(pl.multiple_of(k * width, 128), width)

    def txt_part(k):
        gt_snd[k] = (
            scale * jnp.dot(slope_t[...], zi[:, width_at(k)], preferred_element_type=F32)
        ).astype(BF16)

    def img_part(k):
        gi_snd[k] = (
            scale * jnp.dot(slope[...], zt[:, width_at(k)], preferred_element_type=F32)
        ).astype(BF16)

    class RingSum:
        def __init__(self, snd, mrg, rcv):
            self.snd, self.mrg, self.rcv = snd, mrg, rcv
            h = snd.shape[1] // 2
            self.h, self.a, self.b = h, pl.ds(0, h), pl.ds(h, h)
            self.sems = [slot() for _ in range(6)]

        def far(self):
            send(self.snd.at[xo, self.a], self.rcv.at[0], self.sems[0], XR)
            send(self.snd.at[xo, self.b], self.rcv.at[1], self.sems[1], XL)

        def near(self):
            send(self.snd.at[xr, self.b], self.rcv.at[4], self.sems[4], XR)
            send(self.snd.at[xl, self.a], self.rcv.at[5], self.sems[5], XL)

        def merge(self):
            recv(self.rcv.at[0], self.sems[0])
            self.mrg[0] = (self.rcv[0].astype(F32) + self.snd[xr, self.a].astype(F32)).astype(BF16)
            send(self.mrg.at[0], self.rcv.at[2], self.sems[2], XR)
            recv(self.rcv.at[1], self.sems[1])
            self.mrg[1] = (self.rcv[1].astype(F32) + self.snd[xl, self.b].astype(F32)).astype(BF16)
            send(self.mrg.at[1], self.rcv.at[3], self.sems[3], XL)

        def arrive(self):
            for i in (4, 5, 2, 3):
                recv(self.rcv.at[i], self.sems[i])

        def top(self, start, size):
            at = pl.ds(start, size)
            return self.snd[x, at].astype(F32) + self.rcv[2, at].astype(F32) + self.rcv[5, at].astype(F32)

        def low(self, start, size):
            at = pl.ds(start, size)
            mine = self.snd[x, pl.ds(self.h + start, size)].astype(F32)
            return mine + self.rcv[3, at].astype(F32) + self.rcv[4, at].astype(F32)

    class PairSum:
        def __init__(self, snd, mrg, rcv):
            self.snd, self.mrg, self.rcv = snd, mrg, rcv
            self.sems = [slot() for _ in range(3)]

        def far(self):
            send(self.snd.at[qd], self.rcv.at[0], self.sems[0], PT)

        def near(self):
            send(self.snd.at[qp], self.rcv.at[1], self.sems[1], PT)

        def merge(self):
            recv(self.rcv.at[0], self.sems[0])
            self.mrg[...] = (self.rcv[0].astype(F32) + self.snd[qn].astype(F32)).astype(BF16)
            send(self.mrg, self.rcv.at[2], self.sems[2], YN)

        def arrive(self):
            recv(self.rcv.at[1], self.sems[1])
            recv(self.rcv.at[2], self.sems[2])

        def total(self, start, size):
            at = pl.ds(start, size)
            return self.snd[q, at].astype(F32) + self.rcv[1, at].astype(F32) + self.rcv[2, at].astype(F32)

    st_sem = [slot() for _ in range(6)]
    for i, dev in enumerate((XR, XL, XO)):
        send(stat_t, stt_rcv.at[i], st_sem[i], dev)
    for i, dev in enumerate((PT, YN, DG)):
        send(stat_i, sti_rcv.at[i], st_sem[3 + i], dev)

    txt_sum = RingSum(gt_snd, gt_mrg, gt_rcv)
    img_sum = PairSum(gi_snd, gi_mrg, gi_rcv)
    txt_part(xo)
    txt_sum.far()
    img_part(qd)
    img_sum.far()
    txt_part(xr)
    txt_part(xl)
    txt_sum.near()
    img_part(qn)
    img_sum.merge()
    img_part(qp)
    img_sum.near()
    img_part(q)
    txt_part(x)
    txt_sum.merge()
    for k in range(4):
        xg_t[:, k * rows : (k + 1) * rows] = xg[k].T

    for i in range(3):
        recv(sti_rcv.at[i], st_sem[3 + i])
    stat_tot[...] = stat_i[...] + sti_rcv[0] + sti_rcv[1] + sti_rcv[2]
    row_rad[...] = jnp.broadcast_to(stat_tot[0:1, :], (rows, group)).T
    cost_out[...] = stat_tot[8:9, pl.ds(pl.multiple_of(q * rows, rows), rows)] * (1.0 / total_rows)

    def change(out, unit, inverse, k, column, total):
        at = pl.ds(k * rows, rows)
        u = unit[at, width_at(column)].astype(F32)
        out[at, :] = ((total - u * row_rad[at, 0:1]) * inverse[at, 0:1]).astype(BF16)

    img_sum.arrive()
    for k in range(4):
        change(d_img, zi, inv_i, k, q, img_sum.total(k * rows, rows))

    own_i, own_t = 16 * f_i.shape[1], 16 * f_t.shape[1]
    cut_i, cut_t = own_i - 48, own_t - 64
    part_0 = RingSum(e0_snd, e0_mrg, e0_rcv)
    part_1 = RingSum(e1_snd, e1_mrg, e1_rcv)
    deep = 4 * own_i

    def image_rows(k):
        at = pl.ds(pl.multiple_of(k * deep, 64), deep)
        part = jnp.dot(xg_t[at, :], d_img[...], preferred_element_type=F32).astype(BF16)
        for owner in range(4):
            lo, mid, hi = own_i * owner, own_i * owner + cut_i, own_i * (owner + 1)
            e0_snd[k, cut_i * owner : cut_i * (owner + 1), :] = part[lo:mid]
            e1_snd[k, 48 * owner : 48 * (owner + 1), :] = part[mid:hi]

    image_rows(xo)
    part_0.far()
    image_rows(xr)
    image_rows(xl)
    part_0.near()
    part_1.far()

    for k in range(4):
        tg_t[:, k * rows : (k + 1) * rows] = tg[k].T
    for i in range(3):
        recv(stt_rcv.at[i], st_sem[i])
    txt_total = stat_t[0:1, :] + stt_rcv[0, 0:1, :] + stt_rcv[1, 0:1, :] + stt_rcv[2, 0:1, :]
    row_rad[...] = jnp.broadcast_to(txt_total, (rows, group)).T
    txt_sum.arrive()
    for k in range(2):
        change(d_txt, zt, inv_t, k, x, txt_sum.top(k * rows, rows))
    for k in range(2):
        change(d_txt, zt, inv_t, 2 + k, x, txt_sum.low(k * rows, rows))

    part_t = PairSum(et_snd, et_mrg, et_rcv)
    for k in range(4):
        part = jnp.dot(
            tg_t[4 * own_t * k : 4 * own_t * (k + 1), :], d_txt[...], preferred_element_type=F32
        ).astype(BF16)
        for owner in range(4):
            lo, mid, hi = own_t * owner, own_t * owner + cut_t, own_t * (owner + 1)
            et_snd[owner, cut_t * k : cut_t * (k + 1), :] = part[lo:mid]
            et_snd[owner, 4 * cut_t + 64 * k : 4 * cut_t + 64 * (k + 1), :] = part[mid:hi]
    part_t.far()
    part_t.near()
    part_0.merge()
    part_1.near()
    image_rows(x)
    part_t.merge()
    part_1.merge()

    plus, minus = ring_z // 2, (ring_z - 1) // 2
    own_sem = [slot() for _ in range(12)]

    def units(value):
        return value.reshape(-1, 16, width)

    def at_z(k):
        return pl.ds(2 * lax.rem(k + ring_z, ring_z), 2)

    def to_owners(p):
        plans = {
            0: ((f_i, q, 4, 0, 0, ((qd, DG), (qn, YN), (qp, PT)), 0),),
            1: (
                (f_i, q, 3, 0, 4, ((qd, DG), (qn, YN), (qp, PT)), 3),
                (f_t, x, 1, 12, 0, ((xo, XO), (xr, XR), (xl, XL)), 6),
            ),
            2: ((f_t, x, 4, 0, 1, ((xo, XO), (xr, XR), (xl, XL)), 9),),
        }[p]
        for out, mine, size, base, at, dests, sem in plans:
            for i, (k, dev) in enumerate(dests):
                send(
                    res.at[p, pl.ds(base + size * k, size)], out.at[mine, pl.ds(at, size)],
                    own_sem[sem + i], dev,
                )
            copy = pltpu.make_async_copy(
                res.at[p, pl.ds(base + size * mine, size)], out.at[mine, pl.ds(at, size)],
                loc_sem.at[8 + sem // 3],
            )
            copy.start()
            kept.append(copy)

    kept = []

    def chain(p):
        p_sem = [slot() for _ in range(plus)]
        m_sem = [slot() for _ in range(minus)]
        for s in range(plus):
            value = tile[p, at_z(z + plus - s)]
            if s:
                recv(z_rcv.at[p, s - 1], p_sem[s - 1])
                value = value + z_rcv[p, s - 1].astype(F32)
            z_snd[p, s] = value.astype(BF16)
            send(z_snd.at[p, s], z_rcv.at[p, s], p_sem[s], ZR)
            if s < minus:
                value = tile[p, at_z(z - (minus - s))]
                if s:
                    recv(z_rcv.at[p, plus + s - 1], m_sem[s - 1])
                    value = value + z_rcv[p, plus + s - 1].astype(F32)
                z_snd[p, plus + s] = value.astype(BF16)
                send(z_snd.at[p, plus + s], z_rcv.at[p, plus + s], m_sem[s], ZL)
            yield
        recv(z_rcv.at[p, plus + minus - 1], m_sem[minus - 1])
        recv(z_rcv.at[p, plus - 1], p_sem[plus - 1])
        value = tile[p, at_z(z)] + z_rcv[p, plus - 1].astype(F32) + z_rcv[p, plus + minus - 1].astype(F32)
        y_snd[p] = value.astype(BF16)
        y_sem = slot()
        send(y_snd.at[p], y_rcv.at[p], y_sem, YH)
        yield
        recv(y_rcv.at[p], y_sem)
        res[p, at_z(z)] = (y_snd[p].astype(F32) + y_rcv[p].astype(F32)).astype(BF16)
        p_sem = [slot() for _ in range(plus)]
        m_sem = [slot() for _ in range(minus)]
        for s in range(plus):
            if s:
                recv(res.at[p, at_z(z - s)], p_sem[s - 1])
            send(res.at[p, at_z(z - s)], res.at[p, at_z(z - s)], p_sem[s], ZR)
            if s < minus:
                if s:
                    recv(res.at[p, at_z(z + s)], m_sem[s - 1])
                send(res.at[p, at_z(z + s)], res.at[p, at_z(z + s)], m_sem[s], ZL)
            yield
        recv(res.at[p, at_z(z + minus)], m_sem[minus - 1])
        recv(res.at[p, at_z(z - plus)], p_sem[plus - 1])
        to_owners(p)
        yield

    chains = [chain(p) for p in range(3)]
    part_0.arrive()
    n0, n1 = 4 * cut_i, 4 * 48
    tile[0, 0 : n0 // 32] = units(part_0.top(0, n0 // 2))
    tile[0, n0 // 32 : n0 // 16] = units(part_0.low(0, n0 // 2))
    for p in ORDER:
        if p == "t":
            part_t.arrive()
            tile[1, n1 // 16 : 16] = units(part_t.total(0, 4 * cut_t))
            tile[2] = units(part_t.total(4 * cut_t, 256))
        elif p == "i":
            part_1.arrive()
            tile[1, 0 : n1 // 32] = units(part_1.top(0, n1 // 2))
            tile[1, n1 // 32 : n1 // 16] = units(part_1.low(0, n1 // 2))
        else:
            next(chains[p])

    for i, k in ((2, qp), (1, qn), (0, qd)):
        recv(f_i.at[k, pl.ds(0, 4)], own_sem[i])
        recv(f_i.at[k, pl.ds(4, 3)], own_sem[3 + i])
    for i, k in ((1, xl), (2, xr), (0, xo)):
        recv(f_t.at[k, pl.ds(0, 1)], own_sem[6 + i])
        recv(f_t.at[k, pl.ds(1, 4)], own_sem[9 + i])
    for copy in kept:
        copy.wait()

    for copy in started:
        copy.wait_send()


def widen(cost, images, texts, cost_out, image_out, text_out):
    width = images.shape[-1]
    cost_out[...] = cost[...]
    for k in range(4):
        cols = pl.ds(k * width, width)
        image_out[:, cols] = images[k].reshape(-1, width).astype(F32)
        text_out[:, cols] = texts[k].reshape(-1, width).astype(F32)


def solution(mesh):
    blocks = mesh.shape["blk"]
    ring_z = mesh.shape["dp"] // 2

    def on_device(
        visual_summary_vectors, caption_summary_vectors, pairing_identifiers, valid_sample_tally,
        visual_mapping_matrix, caption_mapping_matrix, sharpness_factor, score_shift_term,
    ):
        rows, deep_i = visual_summary_vectors.shape
        deep_t, embed = caption_mapping_matrix.shape
        group, width = 4 * rows, embed // 4
        own_i, own_t = deep_i // blocks, deep_t // blocks
        vmem = pl.BlockSpec(memory_space=pltpu.VMEM)
        hbm = pl.BlockSpec(memory_space=pl.ANY)
        B = lambda *shape: pltpu.VMEM(shape, BF16)
        F = lambda *shape: pltpu.VMEM(shape, F32)
        n0, n1, nt = 4 * (own_i - 48), 4 * 48, 4 * own_t
        cost, images, texts = pl.pallas_call(
            functools.partial(kernel, blocks * rows, ring_z),
            out_shape=(
                jax.ShapeDtypeStruct((1, rows), F32),
                jax.ShapeDtypeStruct((4, own_i // 16, 16, width), BF16),
                jax.ShapeDtypeStruct((4, own_t // 16, 16, width), BF16),
            ),
            in_specs=[hbm] * 8,
            out_specs=(vmem, hbm, hbm),
            scratch_shapes=[
                pltpu.VMEM((blocks, rows), jnp.int32), pltpu.SMEM((1, blocks), jnp.int32),
                pltpu.SMEM((1,), F32), pltpu.SMEM((1,), F32),
                B(deep_i, embed), B(deep_t, embed), B(4, rows, deep_i), B(4, rows, deep_t),
                B(group, embed), B(group, embed), F(group, rows), F(group, rows), F(rows, embed),
                F(group, rows), F(group, rows), F(group, rows), F(16, group),
                B(group, group), B(group, group), F(16, group), F(8, group),
                F(3, 16, group), F(3, 8, group), F(16, group),
                B(4, group, width), B(2, group // 2, width), B(6, group // 2, width),
                B(4, group, width), B(group, width), B(3, group, width),
                B(group, width), B(group, width), B(deep_i, group), B(deep_t, group),
                B(4, n0, width), B(2, n0 // 2, width), B(6, n0 // 2, width),
                B(4, n1, width), B(2, n1 // 2, width), B(6, n1 // 2, width),
                B(4, nt, width), B(nt, width), B(3, nt, width),
                F(3, 16, 16, width), B(3, ring_z - 1, 2, 16, width), B(3, ring_z - 1, 2, 16, width),
                B(3, 2, 16, width), B(3, 2, 16, width), B(3, 16, 16, width),
                pltpu.SemaphoreType.DMA((12,)),
                pltpu.SemaphoreType.DMA((128,)),
                pltpu.SemaphoreType.DMA((128,)),
            ],
            compiler_params=pltpu.CompilerParams(
                collective_id=0, has_side_effects=True, vmem_limit_bytes=60 * 1024 * 1024
            ),
            name="contrastive_step",
        )(
            pairing_identifiers.reshape(blocks, rows), valid_sample_tally, sharpness_factor, score_shift_term,
            visual_summary_vectors, caption_summary_vectors, visual_mapping_matrix, caption_mapping_matrix,
        )
        cost, grad_image, grad_text = pl.pallas_call(
            widen,
            out_shape=(
                jax.ShapeDtypeStruct((1, rows), F32),
                jax.ShapeDtypeStruct((own_i, embed), F32),
                jax.ShapeDtypeStruct((own_t, embed), F32),
            ),
            in_specs=[vmem] * 3,
            out_specs=(vmem,) * 3,
            name="widen",
        )(cost, images, texts)
        return cost.reshape(rows), grad_image, grad_text

    placed = (
        P(("dp", "blk"), None), P(("dp", "blk"), None), P("dp"), P("dp", None), P(), P(), P(), P(),
    )
    return jax.shard_map(
        on_device,
        mesh=mesh,
        in_specs=placed,
        out_specs=(P(("dp", "blk")), P("blk", None), P("blk", None)),
        check_vma=False,
    )
```

```python
import functools

import jax
import jax.numpy as jnp
from jax import lax
from jax.experimental import pallas as pl
from jax.experimental.pallas import tpu as pltpu
from jax.sharding import PartitionSpec as P

loss_scale = 256.0
epsilon = 1e-06
MESH = pl.DeviceIdType.MESH
F32 = jnp.float32
BF16 = jnp.bfloat16
ORDER = (0, "t", 2, "i", 1) + (0, 2, 1) * 5


def kernel(
    total_rows, ring_z, lab_hbm, tal_hbm, sha_hbm, shi_hbm, x_hbm, t_hbm, wv_hbm, wt_hbm,
    cost_out, f_i, f_t,
    labels, tally, sharp, shift,
    wv, wt, xg, tg, zi, zt, inv_i, inv_t, u_scr, lab_i, row_alive, row_rad, row_cost, col_rad, txt_meta,
    slope, slope_t, stat_i, stat_t, sti_rcv, stt_rcv, stat_tot,
    gt_snd, gt_mrg, gt_rcv, gi_snd, gi_mrg, gi_rcv, d_img, d_txt, xg_t, tg_t,
    e0_snd, e0_mrg, e0_rcv, e1_snd, e1_mrg, e1_rcv, et_snd, et_mrg, et_rcv, tile, z_snd, z_rcv, y_snd, y_rcv, res,
    loc_sem, snd_sem, rcv_sem,
):
    rows = xg.shape[1]
    group = 4 * rows
    embed = zi.shape[1]
    width = embed // 4
    dp, blk = lax.axis_index("dp"), lax.axis_index("blk")
    x, q = lax.div(blk, 4), lax.rem(blk, 4)
    y, c = lax.div(q, 2), lax.rem(q, 2)
    z, yh = lax.rem(dp, ring_z), lax.div(dp, ring_z)
    xr, xl, xo = lax.rem(x + 1, 4), lax.rem(x + 3, 4), lax.rem(x + 2, 4)
    qp, qn, qd = y * 2 + 1 - c, (1 - y) * 2 + c, (1 - y) * 2 + 1 - c
    text_order = (x, xr, xl, xo)
    image_order = (q, qp, qn, qd)
    XR, XL, XO = (dp, xr * 4 + q), (dp, xl * 4 + q), (dp, xo * 4 + q)
    PT, YN, DG = (dp, x * 4 + qp), (dp, x * 4 + qn), (dp, x * 4 + qd)
    Z = {k: (yh * ring_z + lax.rem(z + k + ring_z, ring_z), blk) for k in (1, -1, 2, -2)}
    YH = ((1 - yh) * ring_z + z, blk)

    barrier = pltpu.get_barrier_semaphore()
    peers = (XR, XL, XO, PT, YN, DG, YH, *Z.values())
    for peer in peers:
        pl.semaphore_signal(barrier, inc=1, device_id=peer, device_id_type=MESH)
    loc = [
        pltpu.make_async_copy(t_hbm, tg.at[x], loc_sem.at[0]),
        pltpu.make_async_copy(x_hbm, xg.at[q], loc_sem.at[1]),
        pltpu.make_async_copy(wt_hbm, wt, loc_sem.at[2]),
        pltpu.make_async_copy(wv_hbm, wv, loc_sem.at[3]),
        pltpu.make_async_copy(lab_hbm, labels, loc_sem.at[4]),
        pltpu.make_async_copy(tal_hbm, tally, loc_sem.at[5]),
        pltpu.make_async_copy(sha_hbm, sharp, loc_sem.at[6]),
        pltpu.make_async_copy(shi_hbm, shift, loc_sem.at[7]),
    ]
    for copy in loc:
        copy.start()

    count = [0]
    started = []

    def slot():
        count[0] += 1
        return count[0] - 1

    def send(src, dst, sem, dev):
        copy = pltpu.make_async_remote_copy(
            src_ref=src, dst_ref=dst, send_sem=snd_sem.at[sem], recv_sem=rcv_sem.at[sem],
            device_id=dev, device_id_type=MESH,
        )
        copy.start()
        started.append(copy)

    def recv(dst, sem):
        pltpu.make_async_remote_copy(
            src_ref=dst, dst_ref=dst, send_sem=snd_sem.at[sem], recv_sem=rcv_sem.at[sem],
            device_id=XR, device_id_type=MESH,
        ).wait_recv()

    half = rows // 2
    halves = (pl.ds(0, half), pl.ds(half, half))

    pl.semaphore_wait(barrier, len(peers))
    loc[0].wait()
    t_sem = [slot() for _ in range(6)]
    send(tg.at[x, halves[0]], tg.at[x, halves[0]], t_sem[0], XR)
    send(tg.at[x, halves[1]], tg.at[x, halves[1]], t_sem[1], XL)
    send(tg.at[x, halves[1]], tg.at[x, halves[1]], t_sem[2], XR)
    send(tg.at[x, halves[0]], tg.at[x, halves[0]], t_sem[3], XL)
    loc[1].wait()
    x_sem = [slot() for _ in range(5)]
    for h in range(2):
        send(xg.at[q, halves[h]], xg.at[q, halves[h]], x_sem[h], YN)
    send(xg.at[q], xg.at[q], x_sem[2], PT)

    for copy in loc[4:]:
        copy.wait()
    alive_lane = lax.broadcasted_iota(jnp.int32, (8, rows), 1)
    for k in range(4):
        cols = pl.ds(k * rows, rows)
        block = 4 * text_order[k] + q
        txt_meta[0:8, cols] = jnp.broadcast_to(labels[pl.ds(block, 1), :], (8, rows)).astype(F32)
        txt_meta[8:16, cols] = jnp.where(alive_lane < tally[0, block], 1.0, 0.0)
        block = 4 * x + image_order[k]
        wide = jnp.broadcast_to(labels[pl.ds(block, 1), :].astype(F32), (rows, rows))
        lab_i[pl.ds(k * rows, rows), :] = wide.T

    def project(source, weights, unit, inverse, k, role):
        def body(j, carry):
            cols = pl.ds(pl.multiple_of(j * 512, 512), 512)
            u_scr[:, cols] = jnp.dot(source[k], weights[:, cols], preferred_element_type=F32)
            return carry

        lax.fori_loop(0, embed // 512, body, 0)
        u = u_scr[...]
        inv = 1.0 / jnp.sqrt(jnp.sum(u * u, axis=1, keepdims=True) + epsilon)
        at = pl.ds(role * rows, rows)
        unit[at, :] = (u * inv).astype(BF16)
        inverse[at, :] = jnp.broadcast_to(inv, (rows, rows))

    scale = sharp[0]
    bias = shift[0]

    def pair(first, n_rows, left, n_cols):
        at, cols = pl.ds(first, n_rows), pl.ds(left, n_cols)
        cosine = lax.dot_general(
            zi[at, :], zt[cols, :], (((1,), (1,)), ((), ())), preferred_element_type=F32
        )
        same = lab_i[at, 0:1] == txt_meta[0:1, cols]
        weight = row_alive[at, 0:1] * txt_meta[8:9, cols]
        sign = jnp.where(same, 1.0, -1.0)
        t = -sign * (scale * cosine + bias)
        e = jnp.exp(-jnp.abs(t))
        cost = (jnp.maximum(t, 0.0) + jnp.log1p(e)) * weight
        sigmoid = jnp.where(t >= 0.0, 1.0, e) / (1.0 + e)
        s = -sign * sigmoid * weight * (loss_scale / total_rows)
        s16 = s.astype(BF16)
        slope[at, cols] = s16
        s = s16.astype(F32)
        slope_t[cols, at] = s.T.astype(BF16)
        along = s * cosine * scale
        row_rad[at, :] += jnp.broadcast_to(jnp.sum(along, axis=1, keepdims=True), (n_rows, rows))
        row_cost[at, :] += jnp.broadcast_to(jnp.sum(cost, axis=1, keepdims=True), (n_rows, rows))
        col_rad[0:8, cols] += jnp.broadcast_to(jnp.sum(along, axis=0, keepdims=True), (8, n_cols))

    row_rad[...] = jnp.zeros_like(row_rad)
    row_cost[...] = jnp.zeros_like(row_cost)
    col_rad[...] = jnp.zeros_like(col_rad)
    down = lax.broadcasted_iota(jnp.int32, (rows, rows), 0)
    for k in range(4):
        row_alive[k * rows : (k + 1) * rows, :] = jnp.where(down < tally[0, 4 * x + image_order[k]], 1.0, 0.0)

    loc[2].wait()
    project(tg, wt, zt, inv_t, x, 0)
    recv(tg.at[xl, halves[0]], t_sem[0])
    send(tg.at[xl, halves[0]], tg.at[xl, halves[0]], t_sem[4], XR)
    recv(tg.at[xr, halves[1]], t_sem[1])
    send(tg.at[xr, halves[1]], tg.at[xr, halves[1]], t_sem[5], XL)
    loc[3].wait()
    project(xg, wv, zi, inv_i, q, 0)
    recv(xg.at[qp], x_sem[2])
    recv(xg.at[qn, halves[0]], x_sem[0])
    send(xg.at[qn, halves[0]], xg.at[qn, halves[0]], x_sem[3], PT)
    project(xg, wv, zi, inv_i, qp, 1)
    recv(tg.at[xr, halves[0]], t_sem[3])
    project(tg, wt, zt, inv_t, xr, 1)
    recv(xg.at[qn, halves[1]], x_sem[1])
    send(xg.at[qn, halves[1]], xg.at[qn, halves[1]], x_sem[4], PT)
    recv(tg.at[xl, halves[1]], t_sem[2])
    project(tg, wt, zt, inv_t, xl, 2)
    project(xg, wv, zi, inv_i, qn, 2)
    for k in range(3):
        pair(k * rows, rows, 0, 3 * rows)
    recv(tg.at[xo, halves[0]], t_sem[4])
    recv(tg.at[xo, halves[1]], t_sem[5])
    project(tg, wt, zt, inv_t, xo, 3)
    pair(0, 3 * rows, 3 * rows, rows)
    recv(xg.at[qd, halves[0]], x_sem[3])
    recv(xg.at[qd, halves[1]], x_sem[4])
    project(xg, wv, zi, inv_i, qd, 3)

    pair(3 * rows, rows, 0, group)
    row_t, cost_t = row_rad[...].T, row_cost[...].T
    for k in range(4):
        at = pl.ds(pl.multiple_of(image_order[k] * rows, rows), rows)
        stat_i[0:8, at] = row_t[0:8, k * rows : (k + 1) * rows]
        stat_i[8:16, at] = cost_t[0:8, k * rows : (k + 1) * rows]
        at = pl.ds(pl.multiple_of(text_order[k] * rows, rows), rows)
        stat_t[0:8, at] = col_rad[0:8, k * rows : (k + 1) * rows]

    def width_at(k):
        return pl.ds(pl.multiple_of(k * width, 128), width)

    def txt_part(k):
        part = (scale * jnp.dot(slope_t[...], zi[:, width_at(k)], preferred_element_type=F32)).astype(BF16)
        for r in range(4):
            at = pl.ds(pl.multiple_of(text_order[r] * rows, rows), rows)
            gt_snd[k, at] = part[r * rows : (r + 1) * rows]

    def img_part(k):
        part = (scale * jnp.dot(slope[...], zt[:, width_at(k)], preferred_element_type=F32)).astype(BF16)
        for r in range(4):
            at = pl.ds(pl.multiple_of(image_order[r] * rows, rows), rows)
            gi_snd[k, at] = part[r * rows : (r + 1) * rows]

    class RingSum:
        def __init__(self, snd, mrg, rcv):
            self.snd, self.mrg, self.rcv = snd, mrg, rcv
            h = snd.shape[1] // 2
            self.h, self.a, self.b = h, pl.ds(0, h), pl.ds(h, h)
            self.sems = [slot() for _ in range(6)]

        def far(self):
            send(self.snd.at[xo, self.a], self.rcv.at[0], self.sems[0], XR)
            send(self.snd.at[xo, self.b], self.rcv.at[1], self.sems[1], XL)

        def near(self):
            send(self.snd.at[xr, self.b], self.rcv.at[4], self.sems[4], XR)
            send(self.snd.at[xl, self.a], self.rcv.at[5], self.sems[5], XL)

        def merge(self):
            recv(self.rcv.at[0], self.sems[0])
            self.mrg[0] = (self.rcv[0].astype(F32) + self.snd[xr, self.a].astype(F32)).astype(BF16)
            send(self.mrg.at[0], self.rcv.at[2], self.sems[2], XR)
            recv(self.rcv.at[1], self.sems[1])
            self.mrg[1] = (self.rcv[1].astype(F32) + self.snd[xl, self.b].astype(F32)).astype(BF16)
            send(self.mrg.at[1], self.rcv.at[3], self.sems[3], XL)

        def arrive(self):
            for i in (4, 5, 2, 3):
                recv(self.rcv.at[i], self.sems[i])

        def top(self, start, size):
            at = pl.ds(start, size)
            return self.snd[x, at].astype(F32) + self.rcv[2, at].astype(F32) + self.rcv[5, at].astype(F32)

        def low(self, start, size):
            at = pl.ds(start, size)
            mine = self.snd[x, pl.ds(self.h + start, size)].astype(F32)
            return mine + self.rcv[3, at].astype(F32) + self.rcv[4, at].astype(F32)

    class PairSum:
        def __init__(self, snd, mrg, rcv):
            self.snd, self.mrg, self.rcv = snd, mrg, rcv
            self.sems = [slot() for _ in range(3)]

        def far(self):
            send(self.snd.at[qd], self.rcv.at[0], self.sems[0], PT)

        def near(self):
            send(self.snd.at[qp], self.rcv.at[1], self.sems[1], PT)

        def merge(self):
            recv(self.rcv.at[0], self.sems[0])
            self.mrg[...] = (self.rcv[0].astype(F32) + self.snd[qn].astype(F32)).astype(BF16)
            send(self.mrg, self.rcv.at[2], self.sems[2], YN)

        def arrive(self):
            recv(self.rcv.at[1], self.sems[1])
            recv(self.rcv.at[2], self.sems[2])

        def total(self, start, size):
            at = pl.ds(start, size)
            return self.snd[q, at].astype(F32) + self.rcv[1, at].astype(F32) + self.rcv[2, at].astype(F32)

    st_sem = [slot() for _ in range(6)]
    for i, dev in enumerate((XR, XL, XO)):
        send(stat_t, stt_rcv.at[i], st_sem[i], dev)
    for i, dev in enumerate((PT, YN, DG)):
        send(stat_i, sti_rcv.at[i], st_sem[3 + i], dev)

    txt_sum = RingSum(gt_snd, gt_mrg, gt_rcv)
    img_sum = PairSum(gi_snd, gi_mrg, gi_rcv)
    txt_part(xo)
    txt_sum.far()
    img_part(qd)
    img_sum.far()
    txt_part(xr)
    txt_part(xl)
    txt_sum.near()
    img_part(qn)
    img_sum.merge()
    img_part(qp)
    img_sum.near()
    img_part(q)
    txt_part(x)
    txt_sum.merge()
    for k in range(4):
        xg_t[:, k * rows : (k + 1) * rows] = xg[k].T

    for i in range(3):
        recv(sti_rcv.at[i], st_sem[3 + i])
    stat_tot[...] = stat_i[...] + sti_rcv[0] + sti_rcv[1] + sti_rcv[2]
    row_rad[...] = jnp.broadcast_to(stat_tot[0:1, :], (rows, group)).T
    cost_out[...] = stat_tot[8:9, pl.ds(pl.multiple_of(q * rows, rows), rows)] * (1.0 / total_rows)

    def change(out, unit, inverse, k, role, column, total):
        at = pl.ds(k * rows, rows)
        placed = pl.ds(pl.multiple_of(role * rows, rows), rows)
        u = unit[placed, width_at(column)].astype(F32)
        out[at, :] = ((total - u * row_rad[at, 0:1]) * inverse[placed, 0:1]).astype(BF16)

    def image_role(k):
        return 2 * lax.rem(k // 2 + y, 2) + lax.rem(k % 2 + c, 2)

    def text_role(k):
        ahead = lax.rem(k - x + 4, 4)
        return ahead + lax.div(ahead, 2) * (5 - 2 * ahead)

    img_sum.arrive()
    for k in range(4):
        change(d_img, zi, inv_i, k, image_role(k), q, img_sum.total(k * rows, rows))

    own_i, own_t = 16 * f_i.shape[1], 16 * f_t.shape[1]
    cut_i, cut_t = own_i - 48, own_t - 64
    part_0 = RingSum(e0_snd, e0_mrg, e0_rcv)
    part_1 = RingSum(e1_snd, e1_mrg, e1_rcv)
    deep = 4 * own_i

    def image_rows(k):
        at = pl.ds(pl.multiple_of(k * deep, 64), deep)
        part = jnp.dot(xg_t[at, :], d_img[...], preferred_element_type=F32).astype(BF16)
        for owner in range(4):
            lo, mid, hi = own_i * owner, own_i * owner + cut_i, own_i * (owner + 1)
            e0_snd[k, cut_i * owner : cut_i * (owner + 1), :] = part[lo:mid]
            e1_snd[k, 48 * owner : 48 * (owner + 1), :] = part[mid:hi]

    image_rows(xo)
    part_0.far()
    image_rows(xr)
    image_rows(xl)
    part_0.near()
    part_1.far()

    for k in range(4):
        tg_t[:, k * rows : (k + 1) * rows] = tg[k].T
    for i in range(3):
        recv(stt_rcv.at[i], st_sem[i])
    txt_total = stat_t[0:1, :] + stt_rcv[0, 0:1, :] + stt_rcv[1, 0:1, :] + stt_rcv[2, 0:1, :]
    row_rad[...] = jnp.broadcast_to(txt_total, (rows, group)).T
    txt_sum.arrive()
    for k in range(2):
        change(d_txt, zt, inv_t, k, text_role(k), x, txt_sum.top(k * rows, rows))
    for k in range(2):
        change(d_txt, zt, inv_t, 2 + k, text_role(2 + k), x, txt_sum.low(k * rows, rows))

    part_t = PairSum(et_snd, et_mrg, et_rcv)
    for k in range(4):
        part = jnp.dot(
            tg_t[4 * own_t * k : 4 * own_t * (k + 1), :], d_txt[...], preferred_element_type=F32
        ).astype(BF16)
        for owner in range(4):
            lo, mid, hi = own_t * owner, own_t * owner + cut_t, own_t * (owner + 1)
            et_snd[owner, cut_t * k : cut_t * (k + 1), :] = part[lo:mid]
            et_snd[owner, 4 * cut_t + 64 * k : 4 * cut_t + 64 * (k + 1), :] = part[mid:hi]
    part_t.far()
    part_t.near()
    part_0.merge()
    part_1.near()
    image_rows(x)
    part_t.merge()
    part_1.merge()

    own_sem = [slot() for _ in range(12)]

    def units(value):
        return value.reshape(-1, 16, width)

    def at_z(k):
        return pl.ds(2 * lax.rem(k + ring_z, ring_z), 2)

    def to_owners(p):
        plans = {
            0: ((f_i, q, 4, 0, 0, ((qd, DG), (qn, YN), (qp, PT)), 0),),
            1: (
                (f_i, q, 3, 0, 4, ((qd, DG), (qn, YN), (qp, PT)), 3),
                (f_t, x, 1, 12, 0, ((xo, XO), (xr, XR), (xl, XL)), 6),
            ),
            2: ((f_t, x, 4, 0, 1, ((xo, XO), (xr, XR), (xl, XL)), 9),),
        }[p]
        for out, mine, size, base, at, dests, sem in plans:
            for i, (k, dev) in enumerate(dests):
                send(
                    res.at[p, pl.ds(base + size * k, size)], out.at[mine, pl.ds(at, size)],
                    own_sem[sem + i], dev,
                )
            copy = pltpu.make_async_copy(
                res.at[p, pl.ds(base + size * mine, size)], out.at[mine, pl.ds(at, size)],
                loc_sem.at[8 + sem // 3],
            )
            copy.start()
            kept.append(copy)

    kept = []

    def one_of(k, unit):
        return pl.ds(2 * lax.rem(k + ring_z, ring_z) + unit, 1)

    def chain(p):
        out, got = z_snd.at[p], z_rcv.at[p]
        sems = [slot() for _ in range(8)]
        for i, k in enumerate((4, 3, -3, 1, -1)):
            out[i] = tile[p, at_z(z + k)].astype(BF16)
        send(out.at[0, pl.ds(0, 1)], got.at[0, pl.ds(0, 1)], sems[0], Z[2])
        send(out.at[0, pl.ds(1, 1)], got.at[0, pl.ds(1, 1)], sems[1], Z[-2])
        send(out.at[1], got.at[1], sems[2], Z[1])
        send(out.at[2], got.at[2], sems[3], Z[-1])
        send(out.at[3], got.at[3], sems[4], Z[1])
        send(out.at[4], got.at[4], sems[5], Z[-1])
        yield
        recv(got.at[1], sems[2])
        recv(got.at[0, pl.ds(0, 1)], sems[0])
        out[5] = (tile[p, at_z(z + 2)] + got[1].astype(F32)).astype(BF16)
        out[5, 0:1] = (tile[p, one_of(z + 2, 0)] + got[1, 0:1].astype(F32) + got[0, 0:1].astype(F32)).astype(BF16)
        send(out.at[5], got.at[5], sems[6], Z[2])
        recv(got.at[2], sems[3])
        recv(got.at[0, pl.ds(1, 1)], sems[1])
        out[6] = (tile[p, at_z(z - 2)] + got[2].astype(F32)).astype(BF16)
        out[6, 1:2] = (tile[p, one_of(z - 2, 1)] + got[2, 1:2].astype(F32) + got[0, 1:2].astype(F32)).astype(BF16)
        send(out.at[6], got.at[6], sems[7], Z[-2])
        yield
        for i in (3, 4):
            recv(got.at[i], sems[i + 1])
        value = tile[p, at_z(z)] + got[3].astype(F32) + got[4].astype(F32)
        for i in (5, 6):
            recv(got.at[i], sems[i + 1])
        y_snd[p] = (value + got[5].astype(F32) + got[6].astype(F32)).astype(BF16)
        y_sem = slot()
        send(y_snd.at[p], y_rcv.at[p], y_sem, YH)
        yield
        recv(y_rcv.at[p], y_sem)
        res[p, at_z(z)] = (y_snd[p].astype(F32) + y_rcv[p].astype(F32)).astype(BF16)
        sems = [slot() for _ in range(8)]
        mine = res.at[p, at_z(z)]
        for i, k in enumerate((2, -2, 1, -1)):
            send(mine, mine, sems[i], Z[k])
        yield
        for i, side, unit in ((0, 2, 0), (1, -2, 1)):
            near, part = res.at[p, at_z(z - side)], res.at[p, one_of(z - side, unit)]
            recv(near, sems[i])
            send(part, part, sems[4 + i], Z[side])
            send(near, near, sems[6 + i], Z[side // 2])
        yield
        for i, side, unit in ((0, 2, 0), (1, -2, 1)):
            recv(res.at[p, at_z(z - side // 2)], sems[2 + i])
            recv(res.at[p, one_of(z - 2 * side, unit)], sems[4 + i])
            recv(res.at[p, at_z(z - side - side // 2)], sems[6 + i])
        to_owners(p)
        yield

    chains = [chain(p) for p in range(3)]
    part_0.arrive()
    n0, n1 = 4 * cut_i, 4 * 48
    tile[0, 0 : n0 // 32] = units(part_0.top(0, n0 // 2))
    tile[0, n0 // 32 : n0 // 16] = units(part_0.low(0, n0 // 2))
    for p in ORDER:
        if p == "t":
            part_t.arrive()
            tile[1, n1 // 16 : 16] = units(part_t.total(0, 4 * cut_t))
            tile[2] = units(part_t.total(4 * cut_t, 256))
        elif p == "i":
            part_1.arrive()
            tile[1, 0 : n1 // 32] = units(part_1.top(0, n1 // 2))
            tile[1, n1 // 32 : n1 // 16] = units(part_1.low(0, n1 // 2))
        else:
            next(chains[p])

    for i, k in ((2, qp), (1, qn), (0, qd)):
        recv(f_i.at[k, pl.ds(0, 4)], own_sem[i])
        recv(f_i.at[k, pl.ds(4, 3)], own_sem[3 + i])
    for i, k in ((1, xl), (2, xr), (0, xo)):
        recv(f_t.at[k, pl.ds(0, 1)], own_sem[6 + i])
        recv(f_t.at[k, pl.ds(1, 4)], own_sem[9 + i])
    for copy in kept:
        copy.wait()

    for copy in started:
        copy.wait_send()


def widen(cost, images, texts, cost_out, image_out, text_out):
    width = images.shape[-1]
    cost_out[...] = cost[...]
    for k in range(4):
        cols = pl.ds(k * width, width)
        image_out[:, cols] = images[k].reshape(-1, width).astype(F32)
        text_out[:, cols] = texts[k].reshape(-1, width).astype(F32)


def solution(mesh):
    blocks = mesh.shape["blk"]
    ring_z = mesh.shape["dp"] // 2

    def on_device(
        visual_summary_vectors, caption_summary_vectors, pairing_identifiers, valid_sample_tally,
        visual_mapping_matrix, caption_mapping_matrix, sharpness_factor, score_shift_term,
    ):
        rows, deep_i = visual_summary_vectors.shape
        deep_t, embed = caption_mapping_matrix.shape
        group, width = 4 * rows, embed // 4
        own_i, own_t = deep_i // blocks, deep_t // blocks
        vmem = pl.BlockSpec(memory_space=pltpu.VMEM)
        hbm = pl.BlockSpec(memory_space=pl.ANY)
        B = lambda *shape: pltpu.VMEM(shape, BF16)
        F = lambda *shape: pltpu.VMEM(shape, F32)
        n0, n1, nt = 4 * (own_i - 48), 4 * 48, 4 * own_t
        cost, images, texts = pl.pallas_call(
            functools.partial(kernel, blocks * rows, ring_z),
            out_shape=(
                jax.ShapeDtypeStruct((1, rows), F32),
                jax.ShapeDtypeStruct((4, own_i // 16, 16, width), BF16),
                jax.ShapeDtypeStruct((4, own_t // 16, 16, width), BF16),
            ),
            in_specs=[hbm] * 8,
            out_specs=(vmem, hbm, hbm),
            scratch_shapes=[
                pltpu.VMEM((blocks, rows), jnp.int32), pltpu.SMEM((1, blocks), jnp.int32),
                pltpu.SMEM((1,), F32), pltpu.SMEM((1,), F32),
                B(deep_i, embed), B(deep_t, embed), B(4, rows, deep_i), B(4, rows, deep_t),
                B(group, embed), B(group, embed), F(group, rows), F(group, rows), F(rows, embed),
                F(group, rows), F(group, rows), F(group, rows), F(group, rows), F(8, group), F(16, group),
                B(group, group), B(group, group), F(16, group), F(8, group),
                F(3, 16, group), F(3, 8, group), F(16, group),
                B(4, group, width), B(2, group // 2, width), B(6, group // 2, width),
                B(4, group, width), B(group, width), B(3, group, width),
                B(group, width), B(group, width), B(deep_i, group), B(deep_t, group),
                B(4, n0, width), B(2, n0 // 2, width), B(6, n0 // 2, width),
                B(4, n1, width), B(2, n1 // 2, width), B(6, n1 // 2, width),
                B(4, nt, width), B(nt, width), B(3, nt, width),
                F(3, 16, 16, width), B(3, ring_z - 1, 2, 16, width), B(3, ring_z - 1, 2, 16, width),
                B(3, 2, 16, width), B(3, 2, 16, width), B(3, 16, 16, width),
                pltpu.SemaphoreType.DMA((12,)),
                pltpu.SemaphoreType.DMA((128,)),
                pltpu.SemaphoreType.DMA((128,)),
            ],
            compiler_params=pltpu.CompilerParams(
                collective_id=0, has_side_effects=True, vmem_limit_bytes=60 * 1024 * 1024
            ),
            name="contrastive_step",
        )(
            pairing_identifiers.reshape(blocks, rows), valid_sample_tally, sharpness_factor, score_shift_term,
            visual_summary_vectors, caption_summary_vectors, visual_mapping_matrix, caption_mapping_matrix,
        )
        cost, grad_image, grad_text = pl.pallas_call(
            widen,
            out_shape=(
                jax.ShapeDtypeStruct((1, rows), F32),
                jax.ShapeDtypeStruct((own_i, embed), F32),
                jax.ShapeDtypeStruct((own_t, embed), F32),
            ),
            in_specs=[vmem] * 3,
            out_specs=(vmem,) * 3,
            name="widen",
        )(cost, images, texts)
        return cost.reshape(rows), grad_image, grad_text

    placed = (
        P(("dp", "blk"), None), P(("dp", "blk"), None), P("dp"), P("dp", None), P(), P(), P(), P(),
    )
    return jax.shard_map(
        on_device,
        mesh=mesh,
        in_specs=placed,
        out_specs=(P(("dp", "blk")), P("blk", None), P("blk", None)),
        check_vma=False,
    )
```

```python
import functools

import jax
import jax.numpy as jnp
from jax import lax
from jax.experimental import pallas as pl
from jax.experimental.pallas import tpu as pltpu
from jax.sharding import PartitionSpec as P

loss_scale = 256.0
epsilon = 1e-06
MESH = pl.DeviceIdType.MESH
F32 = jnp.float32
BF16 = jnp.bfloat16
ORDER = (0, "t", 2, "i", 1) + (0, 2, 1) * 5


def kernel(
    total_rows, ring_z, lab_hbm, tal_hbm, sha_hbm, shi_hbm, x_hbm, t_hbm, wv_hbm, wt_hbm,
    cost_out, f_i, f_t,
    labels, tally, sharp, shift,
    wv, wt, xg, tg, zi, zt, inv_i, inv_t, u_scr, lab_i, row_alive, row_rad, row_cost, col_rad, txt_meta,
    slope, slope_t, stat_i, stat_t, sti_rcv, stt_rcv, stat_tot,
    gt_snd, gt_mrg, gt_rcv, gi_snd, gi_mrg, gi_rcv, d_img, d_txt, xg_t, tg_t,
    e0_snd, e0_mrg, e0_rcv, e1_snd, e1_mrg, e1_rcv, et_snd, et_mrg, et_rcv, tile, z_snd, z_rcv, y_snd, y_rcv, res,
    loc_sem, snd_sem, rcv_sem,
):
    rows = xg.shape[1]
    group = 4 * rows
    embed = zi.shape[1]
    width = embed // 4
    dp, blk = lax.axis_index("dp"), lax.axis_index("blk")
    x, q = lax.div(blk, 4), lax.rem(blk, 4)
    y, c = lax.div(q, 2), lax.rem(q, 2)
    z, yh = lax.rem(dp, ring_z), lax.div(dp, ring_z)
    xr, xl, xo = lax.rem(x + 1, 4), lax.rem(x + 3, 4), lax.rem(x + 2, 4)
    qp, qn, qd = y * 2 + 1 - c, (1 - y) * 2 + c, (1 - y) * 2 + 1 - c
    text_order = (x, xr, xl, xo)
    image_order = (q, qp, qn, qd)
    XR, XL, XO = (dp, xr * 4 + q), (dp, xl * 4 + q), (dp, xo * 4 + q)
    PT, YN, DG = (dp, x * 4 + qp), (dp, x * 4 + qn), (dp, x * 4 + qd)
    Z = {k: (yh * ring_z + lax.rem(z + k + ring_z, ring_z), blk) for k in (1, -1, 2, -2)}
    YH = ((1 - yh) * ring_z + z, blk)

    barrier = pltpu.get_barrier_semaphore()
    peers = (XR, XL, XO, PT, YN, DG, YH, *Z.values())
    for peer in peers:
        pl.semaphore_signal(barrier, inc=1, device_id=peer, device_id_type=MESH)
    loc = [
        pltpu.make_async_copy(t_hbm, tg.at[x], loc_sem.at[0]),
        pltpu.make_async_copy(x_hbm, xg.at[q], loc_sem.at[1]),
        pltpu.make_async_copy(wt_hbm, wt, loc_sem.at[2]),
        pltpu.make_async_copy(wv_hbm, wv, loc_sem.at[3]),
        pltpu.make_async_copy(lab_hbm, labels, loc_sem.at[4]),
        pltpu.make_async_copy(tal_hbm, tally, loc_sem.at[5]),
        pltpu.make_async_copy(sha_hbm, sharp, loc_sem.at[6]),
        pltpu.make_async_copy(shi_hbm, shift, loc_sem.at[7]),
    ]
    for copy in loc:
        copy.start()

    count = [0]
    started = []

    def slot():
        count[0] += 1
        return count[0] - 1

    def send(src, dst, sem, dev):
        copy = pltpu.make_async_remote_copy(
            src_ref=src, dst_ref=dst, send_sem=snd_sem.at[sem], recv_sem=rcv_sem.at[sem],
            device_id=dev, device_id_type=MESH,
        )
        copy.start()
        started.append(copy)

    def recv(dst, sem):
        pltpu.make_async_remote_copy(
            src_ref=dst, dst_ref=dst, send_sem=snd_sem.at[sem], recv_sem=rcv_sem.at[sem],
            device_id=XR, device_id_type=MESH,
        ).wait_recv()

    half = rows // 2
    halves = (pl.ds(0, half), pl.ds(half, half))

    pl.semaphore_wait(barrier, len(peers))
    loc[0].wait()
    t_sem = [slot() for _ in range(6)]
    send(tg.at[x, halves[0]], tg.at[x, halves[0]], t_sem[0], XR)
    send(tg.at[x, halves[1]], tg.at[x, halves[1]], t_sem[1], XL)
    send(tg.at[x, halves[1]], tg.at[x, halves[1]], t_sem[2], XR)
    send(tg.at[x, halves[0]], tg.at[x, halves[0]], t_sem[3], XL)
    loc[1].wait()
    x_sem = [slot() for _ in range(5)]
    for h in range(2):
        send(xg.at[q, halves[h]], xg.at[q, halves[h]], x_sem[h], YN)
    send(xg.at[q], xg.at[q], x_sem[2], PT)

    for copy in loc[4:]:
        copy.wait()
    alive_lane = lax.broadcasted_iota(jnp.int32, (8, rows), 1)
    for k in range(4):
        cols = pl.ds(k * rows, rows)
        block = 4 * text_order[k] + q
        txt_meta[0:8, cols] = jnp.broadcast_to(labels[pl.ds(block, 1), :], (8, rows)).astype(F32)
        txt_meta[8:16, cols] = jnp.where(alive_lane < tally[0, block], 1.0, 0.0)
        block = 4 * x + image_order[k]
        wide = jnp.broadcast_to(labels[pl.ds(block, 1), :].astype(F32), (rows, rows))
        lab_i[pl.ds(k * rows, rows), :] = wide.T

    def project(source, weights, unit, inverse, slots, role):
        n_rows = rows * len(slots)
        place = pl.ds(0, n_rows)

        def body(j, carry):
            cols = pl.ds(pl.multiple_of(j * 512, 512), 512)
            left = source[slots[0]] if len(slots) == 1 else jnp.concatenate([source[k] for k in slots], axis=0)
            u_scr[place, cols] = jnp.dot(left, weights[:, cols], preferred_element_type=F32)
            return carry

        lax.fori_loop(0, embed // 512, body, 0)
        u = u_scr[place, :]
        inv = 1.0 / jnp.sqrt(jnp.sum(u * u, axis=1, keepdims=True) + epsilon)
        at = pl.ds(role * rows, n_rows)
        unit[at, :] = (u * inv).astype(BF16)
        inverse[at, :] = jnp.broadcast_to(inv, (n_rows, rows))

    scale = sharp[0]
    bias = shift[0]

    def pair(first, n_rows, left, n_cols):
        at, cols = pl.ds(first, n_rows), pl.ds(left, n_cols)
        cosine = lax.dot_general(
            zi[at, :], zt[cols, :], (((1,), (1,)), ((), ())), preferred_element_type=F32
        )
        same = lab_i[at, 0:1] == txt_meta[0:1, cols]
        weight = row_alive[at, 0:1] * txt_meta[8:9, cols]
        sign = jnp.where(same, 1.0, -1.0)
        t = -sign * (scale * cosine + bias)
        e = jnp.exp(-jnp.abs(t))
        cost = (jnp.maximum(t, 0.0) + jnp.log1p(e)) * weight
        sigmoid = jnp.where(t >= 0.0, 1.0, e) / (1.0 + e)
        s = -sign * sigmoid * weight * (loss_scale / total_rows)
        s16 = s.astype(BF16)
        slope[at, cols] = s16
        s = s16.astype(F32)
        slope_t[cols, at] = s.T.astype(BF16)
        along = s * cosine * scale
        row_rad[at, :] += jnp.broadcast_to(jnp.sum(along, axis=1, keepdims=True), (n_rows, rows))
        row_cost[at, :] += jnp.broadcast_to(jnp.sum(cost, axis=1, keepdims=True), (n_rows, rows))
        col_rad[0:8, cols] += jnp.broadcast_to(jnp.sum(along, axis=0, keepdims=True), (8, n_cols))

    row_rad[...] = jnp.zeros_like(row_rad)
    row_cost[...] = jnp.zeros_like(row_cost)
    col_rad[...] = jnp.zeros_like(col_rad)
    down = lax.broadcasted_iota(jnp.int32, (rows, rows), 0)
    for k in range(4):
        row_alive[k * rows : (k + 1) * rows, :] = jnp.where(down < tally[0, 4 * x + image_order[k]], 1.0, 0.0)

    unit_sem = [slot() for _ in range(4)]

    def role_rows(role):
        return pl.ds(role * rows, rows)

    def share(role, sem):
        send(zi.at[role_rows(role)], zi.at[role_rows(role + 1)], unit_sem[sem], PT)
        send(inv_i.at[role_rows(role)], inv_i.at[role_rows(role + 1)], unit_sem[sem + 1], PT)

    def shared(role, sem):
        recv(zi.at[role_rows(role + 1)], unit_sem[sem])
        recv(inv_i.at[role_rows(role + 1)], unit_sem[sem + 1])

    loc[2].wait()
    project(tg, wt, zt, inv_t, (x,), 0)
    recv(tg.at[xl, halves[0]], t_sem[0])
    send(tg.at[xl, halves[0]], tg.at[xl, halves[0]], t_sem[4], XR)
    recv(tg.at[xr, halves[1]], t_sem[1])
    send(tg.at[xr, halves[1]], tg.at[xr, halves[1]], t_sem[5], XL)
    loc[3].wait()
    project(xg, wv, zi, inv_i, (q,), 0)
    share(0, 0)
    recv(xg.at[qn, halves[0]], x_sem[0])
    send(xg.at[qn, halves[0]], xg.at[qn, halves[0]], x_sem[3], PT)
    shared(0, 0)
    for k in range(2):
        pair(k * rows, rows, 0, rows)
    recv(tg.at[xr, halves[0]], t_sem[3])
    recv(tg.at[xl, halves[1]], t_sem[2])
    project(tg, wt, zt, inv_t, (xr, xl), 1)
    for k in range(2):
        pair(k * rows, rows, rows, 2 * rows)
    recv(xg.at[qn, halves[1]], x_sem[1])
    send(xg.at[qn, halves[1]], xg.at[qn, halves[1]], x_sem[4], PT)
    project(xg, wv, zi, inv_i, (qn,), 2)
    share(2, 2)
    recv(tg.at[xo, halves[0]], t_sem[4])
    recv(tg.at[xo, halves[1]], t_sem[5])
    project(tg, wt, zt, inv_t, (xo,), 3)
    for k in range(2):
        pair(k * rows, rows, 3 * rows, rows)
    pair(2 * rows, rows, 0, group)
    shared(2, 2)

    pair(3 * rows, rows, 0, group)

    def width_at(k):
        return pl.ds(pl.multiple_of(k * width, 128), width)

    def txt_part(k):
        part = (scale * jnp.dot(slope_t[...], zi[:, width_at(k)], preferred_element_type=F32)).astype(BF16)
        for r in range(4):
            at = pl.ds(pl.multiple_of(text_order[r] * rows, rows), rows)
            gt_snd[k, at] = part[r * rows : (r + 1) * rows]

    def img_part(k):
        part = (scale * jnp.dot(slope[...], zt[:, width_at(k)], preferred_element_type=F32)).astype(BF16)
        for r in range(4):
            at = pl.ds(pl.multiple_of(image_order[r] * rows, rows), rows)
            gi_snd[k, at] = part[r * rows : (r + 1) * rows]

    class RingSum:
        def __init__(self, snd, mrg, rcv):
            self.snd, self.mrg, self.rcv = snd, mrg, rcv
            h = snd.shape[1] // 2
            self.h, self.a, self.b = h, pl.ds(0, h), pl.ds(h, h)
            self.sems = [slot() for _ in range(6)]

        def far(self):
            send(self.snd.at[xo, self.a], self.rcv.at[0], self.sems[0], XR)
            send(self.snd.at[xo, self.b], self.rcv.at[1], self.sems[1], XL)

        def near(self):
            send(self.snd.at[xr, self.b], self.rcv.at[4], self.sems[4], XR)
            send(self.snd.at[xl, self.a], self.rcv.at[5], self.sems[5], XL)

        def merge(self):
            recv(self.rcv.at[0], self.sems[0])
            self.mrg[0] = (self.rcv[0].astype(F32) + self.snd[xr, self.a].astype(F32)).astype(BF16)
            send(self.mrg.at[0], self.rcv.at[2], self.sems[2], XR)
            recv(self.rcv.at[1], self.sems[1])
            self.mrg[1] = (self.rcv[1].astype(F32) + self.snd[xl, self.b].astype(F32)).astype(BF16)
            send(self.mrg.at[1], self.rcv.at[3], self.sems[3], XL)

        def arrive(self):
            for i in (4, 5, 2, 3):
                recv(self.rcv.at[i], self.sems[i])

        def top(self, start, size):
            at = pl.ds(start, size)
            return self.snd[x, at].astype(F32) + self.rcv[2, at].astype(F32) + self.rcv[5, at].astype(F32)

        def low(self, start, size):
            at = pl.ds(start, size)
            mine = self.snd[x, pl.ds(self.h + start, size)].astype(F32)
            return mine + self.rcv[3, at].astype(F32) + self.rcv[4, at].astype(F32)

    class PairSum:
        def __init__(self, snd, mrg, rcv):
            self.snd, self.mrg, self.rcv = snd, mrg, rcv
            self.sems = [slot() for _ in range(3)]

        def far(self):
            send(self.snd.at[qd], self.rcv.at[0], self.sems[0], PT)

        def near(self):
            send(self.snd.at[qp], self.rcv.at[1], self.sems[1], PT)

        def merge(self):
            recv(self.rcv.at[0], self.sems[0])
            self.mrg[...] = (self.rcv[0].astype(F32) + self.snd[qn].astype(F32)).astype(BF16)
            send(self.mrg, self.rcv.at[2], self.sems[2], YN)

        def arrive(self):
            recv(self.rcv.at[1], self.sems[1])
            recv(self.rcv.at[2], self.sems[2])

        def total(self, start, size):
            at = pl.ds(start, size)
            return self.snd[q, at].astype(F32) + self.rcv[1, at].astype(F32) + self.rcv[2, at].astype(F32)

    txt_sum = RingSum(gt_snd, gt_mrg, gt_rcv)
    img_sum = PairSum(gi_snd, gi_mrg, gi_rcv)
    txt_part(xo)
    txt_sum.far()
    img_part(qd)
    img_sum.far()
    row_t, cost_t = row_rad[...].T, row_cost[...].T
    for k in range(4):
        at = pl.ds(pl.multiple_of(image_order[k] * rows, rows), rows)
        stat_i[0:8, at] = row_t[0:8, k * rows : (k + 1) * rows]
        stat_i[8:16, at] = cost_t[0:8, k * rows : (k + 1) * rows]
        at = pl.ds(pl.multiple_of(text_order[k] * rows, rows), rows)
        stat_t[0:8, at] = col_rad[0:8, k * rows : (k + 1) * rows]
    st_sem = [slot() for _ in range(6)]
    for i, dev in enumerate((XR, XL, XO)):
        send(stat_t, stt_rcv.at[i], st_sem[i], dev)
    for i, dev in enumerate((PT, YN, DG)):
        send(stat_i, sti_rcv.at[i], st_sem[3 + i], dev)
    txt_part(xr)
    txt_part(xl)
    txt_sum.near()
    img_part(qn)
    img_sum.merge()
    img_part(qp)
    img_sum.near()
    img_part(q)
    txt_part(x)
    txt_sum.merge()
    recv(xg.at[qp], x_sem[2])
    recv(xg.at[qd, halves[0]], x_sem[3])
    recv(xg.at[qd, halves[1]], x_sem[4])
    for k in range(4):
        xg_t[:, k * rows : (k + 1) * rows] = xg[k].T

    for i in range(3):
        recv(sti_rcv.at[i], st_sem[3 + i])
    stat_tot[...] = stat_i[...] + sti_rcv[0] + sti_rcv[1] + sti_rcv[2]
    row_rad[...] = jnp.broadcast_to(stat_tot[0:1, :], (rows, group)).T
    cost_out[...] = stat_tot[8:9, pl.ds(pl.multiple_of(q * rows, rows), rows)] * (1.0 / total_rows)

    def change(out, unit, inverse, k, role, column, total):
        at = pl.ds(k * rows, rows)
        placed = pl.ds(pl.multiple_of(role * rows, rows), rows)
        u = unit[placed, width_at(column)].astype(F32)
        out[at, :] = ((total - u * row_rad[at, 0:1]) * inverse[placed, 0:1]).astype(BF16)

    def image_role(k):
        return 2 * lax.rem(k // 2 + y, 2) + lax.rem(k % 2 + c, 2)

    def text_role(k):
        ahead = lax.rem(k - x + 4, 4)
        return ahead + lax.div(ahead, 2) * (5 - 2 * ahead)

    img_sum.arrive()
    for k in range(4):
        change(d_img, zi, inv_i, k, image_role(k), q, img_sum.total(k * rows, rows))

    own_i, own_t = 16 * f_i.shape[1], 16 * f_t.shape[1]
    cut_i, cut_t = own_i - 48, own_t - 64
    part_0 = RingSum(e0_snd, e0_mrg, e0_rcv)
    part_1 = RingSum(e1_snd, e1_mrg, e1_rcv)
    deep = 4 * own_i

    def image_rows(k):
        at = pl.ds(pl.multiple_of(k * deep, 64), deep)
        part = jnp.dot(xg_t[at, :], d_img[...], preferred_element_type=F32).astype(BF16)
        for owner in range(4):
            lo, mid, hi = own_i * owner, own_i * owner + cut_i, own_i * (owner + 1)
            e0_snd[k, cut_i * owner : cut_i * (owner + 1), :] = part[lo:mid]
            e1_snd[k, 48 * owner : 48 * (owner + 1), :] = part[mid:hi]

    image_rows(xo)
    part_0.far()
    image_rows(xr)
    image_rows(xl)
    part_0.near()
    part_1.far()

    for k in range(4):
        tg_t[:, k * rows : (k + 1) * rows] = tg[k].T
    for i in range(3):
        recv(stt_rcv.at[i], st_sem[i])
    txt_total = stat_t[0:1, :] + stt_rcv[0, 0:1, :] + stt_rcv[1, 0:1, :] + stt_rcv[2, 0:1, :]
    row_rad[...] = jnp.broadcast_to(txt_total, (rows, group)).T
    txt_sum.arrive()
    for k in range(2):
        change(d_txt, zt, inv_t, k, text_role(k), x, txt_sum.top(k * rows, rows))
    for k in range(2):
        change(d_txt, zt, inv_t, 2 + k, text_role(2 + k), x, txt_sum.low(k * rows, rows))

    part_t = PairSum(et_snd, et_mrg, et_rcv)
    for k in range(4):
        part = jnp.dot(
            tg_t[4 * own_t * k : 4 * own_t * (k + 1), :], d_txt[...], preferred_element_type=F32
        ).astype(BF16)
        for owner in range(4):
            lo, mid, hi = own_t * owner, own_t * owner + cut_t, own_t * (owner + 1)
            et_snd[owner, cut_t * k : cut_t * (k + 1), :] = part[lo:mid]
            et_snd[owner, 4 * cut_t + 64 * k : 4 * cut_t + 64 * (k + 1), :] = part[mid:hi]
    part_t.far()
    part_t.near()
    part_0.merge()
    part_1.near()
    image_rows(x)
    part_t.merge()
    part_1.merge()

    own_sem = [slot() for _ in range(12)]

    def units(value):
        return value.reshape(-1, 16, width)

    def at_z(k):
        return pl.ds(2 * lax.rem(k + ring_z, ring_z), 2)

    def to_owners(p):
        plans = {
            0: ((f_i, q, 4, 0, 0, ((qd, DG), (qn, YN), (qp, PT)), 0),),
            1: (
                (f_i, q, 3, 0, 4, ((qd, DG), (qn, YN), (qp, PT)), 3),
                (f_t, x, 1, 12, 0, ((xo, XO), (xr, XR), (xl, XL)), 6),
            ),
            2: ((f_t, x, 4, 0, 1, ((xo, XO), (xr, XR), (xl, XL)), 9),),
        }[p]
        for out, mine, size, base, at, dests, sem in plans:
            for i, (k, dev) in enumerate(dests):
                send(
                    res.at[p, pl.ds(base + size * k, size)], out.at[mine, pl.ds(at, size)],
                    own_sem[sem + i], dev,
                )
            copy = pltpu.make_async_copy(
                res.at[p, pl.ds(base + size * mine, size)], out.at[mine, pl.ds(at, size)],
                loc_sem.at[8 + sem // 3],
            )
            copy.start()
            kept.append(copy)

    kept = []

    def one_of(k, unit):
        return pl.ds(2 * lax.rem(k + ring_z, ring_z) + unit, 1)

    def chain(p):
        out, got = z_snd.at[p], z_rcv.at[p]
        sems = [slot() for _ in range(8)]
        for i, k in enumerate((4, 3, -3, 1, -1)):
            out[i] = tile[p, at_z(z + k)].astype(BF16)
        send(out.at[0, pl.ds(0, 1)], got.at[0, pl.ds(0, 1)], sems[0], Z[2])
        send(out.at[0, pl.ds(1, 1)], got.at[0, pl.ds(1, 1)], sems[1], Z[-2])
        send(out.at[1], got.at[1], sems[2], Z[1])
        send(out.at[2], got.at[2], sems[3], Z[-1])
        send(out.at[3], got.at[3], sems[4], Z[1])
        send(out.at[4], got.at[4], sems[5], Z[-1])
        yield
        recv(got.at[1], sems[2])
        recv(got.at[0, pl.ds(0, 1)], sems[0])
        out[5] = (tile[p, at_z(z + 2)] + got[1].astype(F32)).astype(BF16)
        out[5, 0:1] = (tile[p, one_of(z + 2, 0)] + got[1, 0:1].astype(F32) + got[0, 0:1].astype(F32)).astype(BF16)
        send(out.at[5], got.at[5], sems[6], Z[2])
        recv(got.at[2], sems[3])
        recv(got.at[0, pl.ds(1, 1)], sems[1])
        out[6] = (tile[p, at_z(z - 2)] + got[2].astype(F32)).astype(BF16)
        out[6, 1:2] = (tile[p, one_of(z - 2, 1)] + got[2, 1:2].astype(F32) + got[0, 1:2].astype(F32)).astype(BF16)
        send(out.at[6], got.at[6], sems[7], Z[-2])
        yield
        for i in (3, 4):
            recv(got.at[i], sems[i + 1])
        value = tile[p, at_z(z)] + got[3].astype(F32) + got[4].astype(F32)
        for i in (5, 6):
            recv(got.at[i], sems[i + 1])
        y_snd[p] = (value + got[5].astype(F32) + got[6].astype(F32)).astype(BF16)
        y_sem = slot()
        send(y_snd.at[p], y_rcv.at[p], y_sem, YH)
        yield
        recv(y_rcv.at[p], y_sem)
        res[p, at_z(z)] = (y_snd[p].astype(F32) + y_rcv[p].astype(F32)).astype(BF16)
        sems = [slot() for _ in range(8)]
        mine = res.at[p, at_z(z)]
        for i, k in enumerate((2, -2, 1, -1)):
            send(mine, mine, sems[i], Z[k])
        yield
        for i, side, unit in ((0, 2, 0), (1, -2, 1)):
            near, part = res.at[p, at_z(z - side)], res.at[p, one_of(z - side, unit)]
            recv(near, sems[i])
            send(part, part, sems[4 + i], Z[side])
            send(near, near, sems[6 + i], Z[side // 2])
        yield
        for i, side, unit in ((0, 2, 0), (1, -2, 1)):
            recv(res.at[p, at_z(z - side // 2)], sems[2 + i])
            recv(res.at[p, one_of(z - 2 * side, unit)], sems[4 + i])
            recv(res.at[p, at_z(z - side - side // 2)], sems[6 + i])
        to_owners(p)
        yield

    chains = [chain(p) for p in range(3)]
    part_0.arrive()
    n0, n1 = 4 * cut_i, 4 * 48
    tile[0, 0 : n0 // 32] = units(part_0.top(0, n0 // 2))
    tile[0, n0 // 32 : n0 // 16] = units(part_0.low(0, n0 // 2))
    for p in ORDER:
        if p == "t":
            part_t.arrive()
            tile[1, n1 // 16 : 16] = units(part_t.total(0, 4 * cut_t))
            tile[2] = units(part_t.total(4 * cut_t, 256))
        elif p == "i":
            part_1.arrive()
            tile[1, 0 : n1 // 32] = units(part_1.top(0, n1 // 2))
            tile[1, n1 // 32 : n1 // 16] = units(part_1.low(0, n1 // 2))
        else:
            next(chains[p])

    for i, k in ((2, qp), (1, qn), (0, qd)):
        recv(f_i.at[k, pl.ds(0, 4)], own_sem[i])
        recv(f_i.at[k, pl.ds(4, 3)], own_sem[3 + i])
    for i, k in ((1, xl), (2, xr), (0, xo)):
        recv(f_t.at[k, pl.ds(0, 1)], own_sem[6 + i])
        recv(f_t.at[k, pl.ds(1, 4)], own_sem[9 + i])
    for copy in kept:
        copy.wait()

    for copy in started:
        copy.wait_send()


def widen(cost, images, texts, cost_out, image_out, text_out):
    width = images.shape[-1]
    cost_out[...] = cost[...]
    for k in range(4):
        cols = pl.ds(k * width, width)
        image_out[:, cols] = images[k].reshape(-1, width).astype(F32)
        text_out[:, cols] = texts[k].reshape(-1, width).astype(F32)


def solution(mesh):
    blocks = mesh.shape["blk"]
    ring_z = mesh.shape["dp"] // 2

    def on_device(
        visual_summary_vectors, caption_summary_vectors, pairing_identifiers, valid_sample_tally,
        visual_mapping_matrix, caption_mapping_matrix, sharpness_factor, score_shift_term,
    ):
        rows, deep_i = visual_summary_vectors.shape
        deep_t, embed = caption_mapping_matrix.shape
        group, width = 4 * rows, embed // 4
        own_i, own_t = deep_i // blocks, deep_t // blocks
        vmem = pl.BlockSpec(memory_space=pltpu.VMEM)
        hbm = pl.BlockSpec(memory_space=pl.ANY)
        B = lambda *shape: pltpu.VMEM(shape, BF16)
        F = lambda *shape: pltpu.VMEM(shape, F32)
        n0, n1, nt = 4 * (own_i - 48), 4 * 48, 4 * own_t
        cost, images, texts = pl.pallas_call(
            functools.partial(kernel, blocks * rows, ring_z),
            out_shape=(
                jax.ShapeDtypeStruct((1, rows), F32),
                jax.ShapeDtypeStruct((4, own_i // 16, 16, width), BF16),
                jax.ShapeDtypeStruct((4, own_t // 16, 16, width), BF16),
            ),
            in_specs=[hbm] * 8,
            out_specs=(vmem, hbm, hbm),
            scratch_shapes=[
                pltpu.VMEM((blocks, rows), jnp.int32), pltpu.SMEM((1, blocks), jnp.int32),
                pltpu.SMEM((1,), F32), pltpu.SMEM((1,), F32),
                B(deep_i, embed), B(deep_t, embed), B(4, rows, deep_i), B(4, rows, deep_t),
                B(group, embed), B(group, embed), F(group, rows), F(group, rows), F(2 * rows, embed),
                F(group, rows), F(group, rows), F(group, rows), F(group, rows), F(8, group), F(16, group),
                B(group, group), B(group, group), F(16, group), F(8, group),
                F(3, 16, group), F(3, 8, group), F(16, group),
                B(4, group, width), B(2, group // 2, width), B(6, group // 2, width),
                B(4, group, width), B(group, width), B(3, group, width),
                B(group, width), B(group, width), B(deep_i, group), B(deep_t, group),
                B(4, n0, width), B(2, n0 // 2, width), B(6, n0 // 2, width),
                B(4, n1, width), B(2, n1 // 2, width), B(6, n1 // 2, width),
                B(4, nt, width), B(nt, width), B(3, nt, width),
                F(3, 16, 16, width), B(3, ring_z - 1, 2, 16, width), B(3, ring_z - 1, 2, 16, width),
                B(3, 2, 16, width), B(3, 2, 16, width), B(3, 16, 16, width),
                pltpu.SemaphoreType.DMA((12,)),
                pltpu.SemaphoreType.DMA((128,)),
                pltpu.SemaphoreType.DMA((128,)),
            ],
            compiler_params=pltpu.CompilerParams(
                collective_id=0, has_side_effects=True, vmem_limit_bytes=60 * 1024 * 1024
            ),
            name="contrastive_step",
        )(
            pairing_identifiers.reshape(blocks, rows), valid_sample_tally, sharpness_factor, score_shift_term,
            visual_summary_vectors, caption_summary_vectors, visual_mapping_matrix, caption_mapping_matrix,
        )
        cost, grad_image, grad_text = pl.pallas_call(
            widen,
            out_shape=(
                jax.ShapeDtypeStruct((1, rows), F32),
                jax.ShapeDtypeStruct((own_i, embed), F32),
                jax.ShapeDtypeStruct((own_t, embed), F32),
            ),
            in_specs=[vmem] * 3,
            out_specs=(vmem,) * 3,
            name="widen",
        )(cost, images, texts)
        return cost.reshape(rows), grad_image, grad_text

    placed = (
        P(("dp", "blk"), None), P(("dp", "blk"), None), P("dp"), P("dp", None), P(), P(), P(), P(),
    )
    return jax.shard_map(
        on_device,
        mesh=mesh,
        in_specs=placed,
        out_specs=(P(("dp", "blk")), P("blk", None), P("blk", None)),
        check_vma=False,
    )
```

```python
import functools

import jax
import jax.numpy as jnp
from jax import lax
from jax.experimental import pallas as pl
from jax.experimental.pallas import tpu as pltpu
from jax.sharding import PartitionSpec as P

loss_scale = 256.0
epsilon = 1e-06
MESH = pl.DeviceIdType.MESH
F32 = jnp.float32
BF16 = jnp.bfloat16
ORDER = (0, "t", 2, "i", 1) + (0, 1, 2) * 5


def kernel(
    total_rows, ring_z, lab_hbm, tal_hbm, sha_hbm, shi_hbm, x_hbm, t_hbm, wv_hbm, wt_hbm,
    cost_out, f_i, f_t,
    labels, tally, sharp, shift, cost_own,
    wv, wt, xg, tg, zi, zt, inv_i, inv_t, u_scr, lab_i, row_alive, row_rad, row_cost, col_rad, txt_meta,
    slope, slope_t, stat_i, stat_t, sti_rcv, stt_rcv, stat_tot,
    gt_snd, gt_mrg, gt_rcv, gi_snd, gi_mrg, gi_rcv, d_img, d_txt, xg_t, tg_t,
    e0_snd, e0_mrg, e0_rcv, e1_snd, e1_mrg, e1_rcv, et_snd, et_mrg, et_rcv, tile, z_snd, z_rcv, y_snd, y_rcv, res,
    loc_sem, snd_sem, rcv_sem,
):
    rows = xg.shape[1]
    group = 4 * rows
    embed = zi.shape[1]
    width = embed // 4
    dp, blk = lax.axis_index("dp"), lax.axis_index("blk")
    x, q = lax.div(blk, 4), lax.rem(blk, 4)
    y, c = lax.div(q, 2), lax.rem(q, 2)
    z, yh = lax.rem(dp, ring_z), lax.div(dp, ring_z)
    xr, xl, xo = lax.rem(x + 1, 4), lax.rem(x + 3, 4), lax.rem(x + 2, 4)
    qp, qn, qd = y * 2 + 1 - c, (1 - y) * 2 + c, (1 - y) * 2 + 1 - c
    text_order = (x, xr, xl, xo)
    image_order = (q, qp, qn, qd)
    XR, XL, XO = (dp, xr * 4 + q), (dp, xl * 4 + q), (dp, xo * 4 + q)
    PT, YN, DG = (dp, x * 4 + qp), (dp, x * 4 + qn), (dp, x * 4 + qd)
    Z = {k: (yh * ring_z + lax.rem(z + k + ring_z, ring_z), blk) for k in (1, -1, 2, -2)}
    YH = ((1 - yh) * ring_z + z, blk)

    barrier = pltpu.get_barrier_semaphore()
    peers = (XR, XL, XO, PT, YN, DG, YH, *Z.values())
    for peer in peers:
        pl.semaphore_signal(barrier, inc=1, device_id=peer, device_id_type=MESH)
    loc = [
        pltpu.make_async_copy(t_hbm, tg.at[x], loc_sem.at[0]),
        pltpu.make_async_copy(x_hbm, xg.at[q], loc_sem.at[1]),
        pltpu.make_async_copy(wt_hbm, wt, loc_sem.at[2]),
        pltpu.make_async_copy(wv_hbm, wv, loc_sem.at[3]),
        pltpu.make_async_copy(lab_hbm, labels, loc_sem.at[4]),
        pltpu.make_async_copy(tal_hbm, tally, loc_sem.at[5]),
        pltpu.make_async_copy(sha_hbm, sharp, loc_sem.at[6]),
        pltpu.make_async_copy(shi_hbm, shift, loc_sem.at[7]),
    ]
    for copy in loc:
        copy.start()

    count = [0]
    started = []

    def slot():
        count[0] += 1
        return count[0] - 1

    def send(src, dst, sem, dev):
        copy = pltpu.make_async_remote_copy(
            src_ref=src, dst_ref=dst, send_sem=snd_sem.at[sem], recv_sem=rcv_sem.at[sem],
            device_id=dev, device_id_type=MESH,
        )
        copy.start()
        started.append(copy)

    def recv(dst, sem):
        pltpu.make_async_remote_copy(
            src_ref=dst, dst_ref=dst, send_sem=snd_sem.at[sem], recv_sem=rcv_sem.at[sem],
            device_id=XR, device_id_type=MESH,
        ).wait_recv()

    half = rows // 2
    halves = (pl.ds(0, half), pl.ds(half, half))

    pl.semaphore_wait(barrier, len(peers))
    loc[0].wait()
    t_sem = [slot() for _ in range(6)]
    send(tg.at[x, halves[0]], tg.at[x, halves[0]], t_sem[0], XR)
    send(tg.at[x, halves[1]], tg.at[x, halves[1]], t_sem[1], XL)
    send(tg.at[x, halves[1]], tg.at[x, halves[1]], t_sem[2], XR)
    send(tg.at[x, halves[0]], tg.at[x, halves[0]], t_sem[3], XL)
    loc[1].wait()
    x_sem = [slot() for _ in range(5)]
    for h in range(2):
        send(xg.at[q, halves[h]], xg.at[q, halves[h]], x_sem[h], YN)
    send(xg.at[q], xg.at[q], x_sem[2], PT)

    for copy in loc[4:]:
        copy.wait()
    alive_lane = lax.broadcasted_iota(jnp.int32, (8, rows), 1)
    for k in range(4):
        cols = pl.ds(k * rows, rows)
        block = 4 * text_order[k] + q
        txt_meta[0:8, cols] = jnp.broadcast_to(labels[pl.ds(block, 1), :], (8, rows)).astype(F32)
        txt_meta[8:16, cols] = jnp.where(alive_lane < tally[0, block], 1.0, 0.0)
        block = 4 * x + image_order[k]
        wide = jnp.broadcast_to(labels[pl.ds(block, 1), :].astype(F32), (rows, rows))
        lab_i[pl.ds(k * rows, rows), :] = wide.T

    def project(source, weights, unit, inverse, slots, role):
        n_rows = rows * len(slots)
        place = pl.ds(0, n_rows)

        def body(j, carry):
            cols = pl.ds(pl.multiple_of(j * 512, 512), 512)
            left = source[slots[0]] if len(slots) == 1 else jnp.concatenate([source[k] for k in slots], axis=0)
            u_scr[place, cols] = jnp.dot(left, weights[:, cols], preferred_element_type=F32)
            return carry

        lax.fori_loop(0, embed // 512, body, 0)
        u = u_scr[place, :]
        inv = 1.0 / jnp.sqrt(jnp.sum(u * u, axis=1, keepdims=True) + epsilon)
        at = pl.ds(role * rows, n_rows)
        unit[at, :] = (u * inv).astype(BF16)
        inverse[at, :] = jnp.broadcast_to(inv, (n_rows, rows))

    scale = sharp[0]
    bias = shift[0]

    def pair(first, n_rows, left, n_cols):
        at, cols = pl.ds(first, n_rows), pl.ds(left, n_cols)
        cosine = lax.dot_general(
            zi[at, :], zt[cols, :], (((1,), (1,)), ((), ())), preferred_element_type=F32
        )
        same = lab_i[at, 0:1] == txt_meta[0:1, cols]
        weight = row_alive[at, 0:1] * txt_meta[8:9, cols]
        sign = jnp.where(same, 1.0, -1.0)
        t = -sign * (scale * cosine + bias)
        e = jnp.exp(-jnp.abs(t))
        cost = (jnp.maximum(t, 0.0) + jnp.log1p(e)) * weight
        sigmoid = jnp.where(t >= 0.0, 1.0, e) / (1.0 + e)
        s = -sign * sigmoid * weight * (loss_scale / total_rows)
        s16 = s.astype(BF16)
        slope[at, cols] = s16
        s = s16.astype(F32)
        slope_t[cols, at] = s.T.astype(BF16)
        along = s * cosine * scale
        row_rad[at, :] += jnp.broadcast_to(jnp.sum(along, axis=1, keepdims=True), (n_rows, rows))
        row_cost[at, :] += jnp.broadcast_to(jnp.sum(cost, axis=1, keepdims=True), (n_rows, rows))
        col_rad[0:8, cols] += jnp.broadcast_to(jnp.sum(along, axis=0, keepdims=True), (8, n_cols))

    row_rad[...] = jnp.zeros_like(row_rad)
    row_cost[...] = jnp.zeros_like(row_cost)
    col_rad[...] = jnp.zeros_like(col_rad)
    down = lax.broadcasted_iota(jnp.int32, (rows, rows), 0)
    for k in range(4):
        row_alive[k * rows : (k + 1) * rows, :] = jnp.where(down < tally[0, 4 * x + image_order[k]], 1.0, 0.0)

    unit_sem = [slot() for _ in range(4)]

    def role_rows(role):
        return pl.ds(role * rows, rows)

    def share(role, sem):
        send(zi.at[role_rows(role)], zi.at[role_rows(role + 1)], unit_sem[sem], PT)
        send(inv_i.at[role_rows(role)], inv_i.at[role_rows(role + 1)], unit_sem[sem + 1], PT)

    def shared(role, sem):
        recv(zi.at[role_rows(role + 1)], unit_sem[sem])
        recv(inv_i.at[role_rows(role + 1)], unit_sem[sem + 1])

    loc[2].wait()
    project(tg, wt, zt, inv_t, (x,), 0)
    recv(tg.at[xl, halves[0]], t_sem[0])
    send(tg.at[xl, halves[0]], tg.at[xl, halves[0]], t_sem[4], XR)
    recv(tg.at[xr, halves[1]], t_sem[1])
    send(tg.at[xr, halves[1]], tg.at[xr, halves[1]], t_sem[5], XL)
    loc[3].wait()
    project(xg, wv, zi, inv_i, (q,), 0)
    share(0, 0)
    recv(xg.at[qn, halves[0]], x_sem[0])
    send(xg.at[qn, halves[0]], xg.at[qn, halves[0]], x_sem[3], PT)
    shared(0, 0)
    for k in range(2):
        pair(k * rows, rows, 0, rows)
    recv(tg.at[xr, halves[0]], t_sem[3])
    recv(tg.at[xl, halves[1]], t_sem[2])
    project(tg, wt, zt, inv_t, (xr, xl), 1)
    for k in range(2):
        pair(k * rows, rows, rows, 2 * rows)
    recv(xg.at[qn, halves[1]], x_sem[1])
    send(xg.at[qn, halves[1]], xg.at[qn, halves[1]], x_sem[4], PT)
    project(xg, wv, zi, inv_i, (qn,), 2)
    share(2, 2)
    recv(tg.at[xo, halves[0]], t_sem[4])
    recv(tg.at[xo, halves[1]], t_sem[5])
    project(tg, wt, zt, inv_t, (xo,), 3)
    for k in range(2):
        pair(k * rows, rows, 3 * rows, rows)
    pair(2 * rows, rows, 0, group)
    shared(2, 2)

    pair(3 * rows, rows, 0, group)

    def width_at(k):
        return pl.ds(pl.multiple_of(k * width, 128), width)

    def txt_part(k):
        part = (scale * jnp.dot(slope_t[...], zi[:, width_at(k)], preferred_element_type=F32)).astype(BF16)
        for r in range(4):
            at = pl.ds(pl.multiple_of(text_order[r] * rows, rows), rows)
            gt_snd[k, at] = part[r * rows : (r + 1) * rows]

    def img_part(k):
        part = (scale * jnp.dot(slope[...], zt[:, width_at(k)], preferred_element_type=F32)).astype(BF16)
        for r in range(4):
            at = pl.ds(pl.multiple_of(image_order[r] * rows, rows), rows)
            gi_snd[k, at] = part[r * rows : (r + 1) * rows]

    class RingSum:
        def __init__(self, snd, mrg, rcv):
            self.snd, self.mrg, self.rcv = snd, mrg, rcv
            h = snd.shape[1] // 2
            self.h, self.a, self.b = h, pl.ds(0, h), pl.ds(h, h)
            self.sems = [slot() for _ in range(6)]

        def far(self):
            send(self.snd.at[xo, self.a], self.rcv.at[0], self.sems[0], XR)
            send(self.snd.at[xo, self.b], self.rcv.at[1], self.sems[1], XL)

        def near(self):
            send(self.snd.at[xr, self.b], self.rcv.at[4], self.sems[4], XR)
            send(self.snd.at[xl, self.a], self.rcv.at[5], self.sems[5], XL)

        def merge(self):
            recv(self.rcv.at[0], self.sems[0])
            self.mrg[0] = (self.rcv[0].astype(F32) + self.snd[xr, self.a].astype(F32)).astype(BF16)
            send(self.mrg.at[0], self.rcv.at[2], self.sems[2], XR)
            recv(self.rcv.at[1], self.sems[1])
            self.mrg[1] = (self.rcv[1].astype(F32) + self.snd[xl, self.b].astype(F32)).astype(BF16)
            send(self.mrg.at[1], self.rcv.at[3], self.sems[3], XL)

        def arrive(self):
            for i in (4, 5, 2, 3):
                recv(self.rcv.at[i], self.sems[i])

        def top(self, start, size):
            at = pl.ds(start, size)
            return self.snd[x, at].astype(F32) + self.rcv[2, at].astype(F32) + self.rcv[5, at].astype(F32)

        def low(self, start, size):
            at = pl.ds(start, size)
            mine = self.snd[x, pl.ds(self.h + start, size)].astype(F32)
            return mine + self.rcv[3, at].astype(F32) + self.rcv[4, at].astype(F32)

    class PairSum:
        def __init__(self, snd, mrg, rcv):
            self.snd, self.mrg, self.rcv = snd, mrg, rcv
            self.sems = [slot() for _ in range(3)]

        def far(self):
            send(self.snd.at[qd], self.rcv.at[0], self.sems[0], PT)

        def near(self):
            send(self.snd.at[qp], self.rcv.at[1], self.sems[1], PT)

        def merge(self):
            recv(self.rcv.at[0], self.sems[0])
            self.mrg[...] = (self.rcv[0].astype(F32) + self.snd[qn].astype(F32)).astype(BF16)
            send(self.mrg, self.rcv.at[2], self.sems[2], YN)

        def arrive(self):
            recv(self.rcv.at[1], self.sems[1])
            recv(self.rcv.at[2], self.sems[2])

        def total(self, start, size):
            at = pl.ds(start, size)
            return self.snd[q, at].astype(F32) + self.rcv[1, at].astype(F32) + self.rcv[2, at].astype(F32)

    txt_sum = RingSum(gt_snd, gt_mrg, gt_rcv)
    img_sum = PairSum(gi_snd, gi_mrg, gi_rcv)
    txt_part(xo)
    txt_sum.far()
    img_part(qd)
    img_sum.far()
    row_t, cost_t = row_rad[...].T, row_cost[...].T
    for k in range(4):
        at = pl.ds(pl.multiple_of(image_order[k] * rows, rows), rows)
        stat_i[0:8, at] = row_t[0:8, k * rows : (k + 1) * rows]
        stat_i[8:16, at] = cost_t[0:8, k * rows : (k + 1) * rows]
        at = pl.ds(pl.multiple_of(text_order[k] * rows, rows), rows)
        stat_t[0:8, at] = col_rad[0:8, k * rows : (k + 1) * rows]
    st_sem = [slot() for _ in range(6)]
    for i, dev in enumerate((XR, XL, XO)):
        send(stat_t, stt_rcv.at[i], st_sem[i], dev)
    for i, dev in enumerate((PT, YN, DG)):
        send(stat_i, sti_rcv.at[i], st_sem[3 + i], dev)
    txt_part(xr)
    txt_part(xl)
    txt_sum.near()
    img_part(qn)
    img_sum.merge()
    img_part(qp)
    img_sum.near()
    img_part(q)
    txt_part(x)
    txt_sum.merge()
    recv(xg.at[qp], x_sem[2])
    recv(xg.at[qd, halves[0]], x_sem[3])
    recv(xg.at[qd, halves[1]], x_sem[4])
    for k in range(4):
        xg_t[:, k * rows : (k + 1) * rows] = xg[k].T

    for i in range(3):
        recv(sti_rcv.at[i], st_sem[3 + i])
    stat_tot[...] = stat_i[...] + sti_rcv[0] + sti_rcv[1] + sti_rcv[2]
    row_rad[...] = jnp.broadcast_to(stat_tot[0:1, :], (rows, group)).T
    cost_own[...] = stat_tot[8:9, pl.ds(pl.multiple_of(q * rows, rows), rows)] * (1.0 / total_rows)
    cost_copy = pltpu.make_async_copy(cost_own, cost_out, loc_sem.at[12])
    cost_copy.start()

    def change(out, unit, inverse, k, role, column, total):
        at = pl.ds(k * rows, rows)
        placed = pl.ds(pl.multiple_of(role * rows, rows), rows)
        u = unit[placed, width_at(column)].astype(F32)
        out[at, :] = ((total - u * row_rad[at, 0:1]) * inverse[placed, 0:1]).astype(BF16)

    def image_role(k):
        return 2 * lax.rem(k // 2 + y, 2) + lax.rem(k % 2 + c, 2)

    def text_role(k):
        ahead = lax.rem(k - x + 4, 4)
        return ahead + lax.div(ahead, 2) * (5 - 2 * ahead)

    img_sum.arrive()
    for k in range(4):
        change(d_img, zi, inv_i, k, image_role(k), q, img_sum.total(k * rows, rows))

    own_i, own_t = 16 * f_i.shape[1], 16 * f_t.shape[1]
    cut_i, cut_t = own_i - 48, own_t - 64
    part_0 = RingSum(e0_snd, e0_mrg, e0_rcv)
    part_1 = RingSum(e1_snd, e1_mrg, e1_rcv)
    deep = 4 * own_i

    def image_rows(k):
        at = pl.ds(pl.multiple_of(k * deep, 64), deep)
        part = jnp.dot(xg_t[at, :], d_img[...], preferred_element_type=F32).astype(BF16)
        for owner in range(4):
            lo, mid, hi = own_i * owner, own_i * owner + cut_i, own_i * (owner + 1)
            e0_snd[k, cut_i * owner : cut_i * (owner + 1), :] = part[lo:mid]
            e1_snd[k, 48 * owner : 48 * (owner + 1), :] = part[mid:hi]

    image_rows(xo)
    part_0.far()
    image_rows(xr)
    image_rows(xl)
    part_0.near()
    part_1.far()

    for k in range(4):
        tg_t[:, k * rows : (k + 1) * rows] = tg[k].T
    for i in range(3):
        recv(stt_rcv.at[i], st_sem[i])
    txt_total = stat_t[0:1, :] + stt_rcv[0, 0:1, :] + stt_rcv[1, 0:1, :] + stt_rcv[2, 0:1, :]
    row_rad[...] = jnp.broadcast_to(txt_total, (rows, group)).T
    txt_sum.arrive()
    for k in range(2):
        change(d_txt, zt, inv_t, k, text_role(k), x, txt_sum.top(k * rows, rows))
    for k in range(2):
        change(d_txt, zt, inv_t, 2 + k, text_role(2 + k), x, txt_sum.low(k * rows, rows))

    part_t = PairSum(et_snd, et_mrg, et_rcv)
    for k in range(4):
        part = jnp.dot(
            tg_t[4 * own_t * k : 4 * own_t * (k + 1), :], d_txt[...], preferred_element_type=F32
        ).astype(BF16)
        for owner in range(4):
            lo, mid, hi = own_t * owner, own_t * owner + cut_t, own_t * (owner + 1)
            et_snd[owner, cut_t * k : cut_t * (k + 1), :] = part[lo:mid]
            et_snd[owner, 4 * cut_t + 64 * k : 4 * cut_t + 64 * (k + 1), :] = part[mid:hi]
    part_t.far()
    part_t.near()
    part_0.merge()
    part_1.near()
    image_rows(x)
    part_t.merge()
    part_1.merge()

    own_sem = [slot() for _ in range(12)]

    def units(value):
        return value.reshape(-1, 16, width)

    def at_z(k):
        return pl.ds(2 * lax.rem(k + ring_z, ring_z), 2)

    def to_owners(p):
        plans = {
            0: ((f_i, q, 4, 0, 0, ((qd, DG), (qn, YN), (qp, PT)), 0),),
            1: (
                (f_i, q, 3, 0, 4, ((qd, DG), (qn, YN), (qp, PT)), 3),
                (f_t, x, 1, 12, 0, ((xo, XO), (xr, XR), (xl, XL)), 6),
            ),
            2: ((f_t, x, 4, 0, 1, ((xo, XO), (xr, XR), (xl, XL)), 9),),
        }[p]
        for out, mine, size, base, at, dests, sem in plans:
            for i, (k, dev) in enumerate(dests):
                send(
                    res.at[p, pl.ds(base + size * k, size)], out.at[mine, pl.ds(at, size)],
                    own_sem[sem + i], dev,
                )
            copy = pltpu.make_async_copy(
                res.at[p, pl.ds(base + size * mine, size)], out.at[mine, pl.ds(at, size)],
                loc_sem.at[8 + sem // 3],
            )
            copy.start()
            kept.append(copy)

    kept = []

    def one_of(k, unit):
        return pl.ds(2 * lax.rem(k + ring_z, ring_z) + unit, 1)

    def chain(p):
        out, got = z_snd.at[p], z_rcv.at[p]
        sems = [slot() for _ in range(8)]
        for i, k in enumerate((4, 3, -3, 1, -1)):
            out[i] = tile[p, at_z(z + k)].astype(BF16)
        send(out.at[0, pl.ds(0, 1)], got.at[0, pl.ds(0, 1)], sems[0], Z[2])
        send(out.at[0, pl.ds(1, 1)], got.at[0, pl.ds(1, 1)], sems[1], Z[-2])
        send(out.at[1], got.at[1], sems[2], Z[1])
        send(out.at[2], got.at[2], sems[3], Z[-1])
        send(out.at[3], got.at[3], sems[4], Z[1])
        send(out.at[4], got.at[4], sems[5], Z[-1])
        yield
        recv(got.at[1], sems[2])
        recv(got.at[0, pl.ds(0, 1)], sems[0])
        out[5] = (tile[p, at_z(z + 2)] + got[1].astype(F32)).astype(BF16)
        out[5, 0:1] = (tile[p, one_of(z + 2, 0)] + got[1, 0:1].astype(F32) + got[0, 0:1].astype(F32)).astype(BF16)
        send(out.at[5], got.at[5], sems[6], Z[2])
        recv(got.at[2], sems[3])
        recv(got.at[0, pl.ds(1, 1)], sems[1])
        out[6] = (tile[p, at_z(z - 2)] + got[2].astype(F32)).astype(BF16)
        out[6, 1:2] = (tile[p, one_of(z - 2, 1)] + got[2, 1:2].astype(F32) + got[0, 1:2].astype(F32)).astype(BF16)
        send(out.at[6], got.at[6], sems[7], Z[-2])
        yield
        for i in (3, 4):
            recv(got.at[i], sems[i + 1])
        value = tile[p, at_z(z)] + got[3].astype(F32) + got[4].astype(F32)
        for i in (5, 6):
            recv(got.at[i], sems[i + 1])
        y_snd[p] = (value + got[5].astype(F32) + got[6].astype(F32)).astype(BF16)
        y_sem = slot()
        send(y_snd.at[p], y_rcv.at[p], y_sem, YH)
        yield
        recv(y_rcv.at[p], y_sem)
        res[p, at_z(z)] = (y_snd[p].astype(F32) + y_rcv[p].astype(F32)).astype(BF16)
        sems = [slot() for _ in range(8)]
        mine = res.at[p, at_z(z)]
        for i, k in enumerate((2, -2, 1, -1)):
            send(mine, mine, sems[i], Z[k])
        yield
        for i, side, unit in ((0, 2, 0), (1, -2, 1)):
            near, part = res.at[p, at_z(z - side)], res.at[p, one_of(z - side, unit)]
            recv(near, sems[i])
            send(part, part, sems[4 + i], Z[side])
            send(near, near, sems[6 + i], Z[side // 2])
        yield
        for i, side, unit in ((0, 2, 0), (1, -2, 1)):
            recv(res.at[p, at_z(z - side // 2)], sems[2 + i])
            recv(res.at[p, one_of(z - 2 * side, unit)], sems[4 + i])
            recv(res.at[p, at_z(z - side - side // 2)], sems[6 + i])
        to_owners(p)
        yield

    chains = [chain(p) for p in range(3)]
    part_0.arrive()
    n0, n1 = 4 * cut_i, 4 * 48
    tile[0, 0 : n0 // 32] = units(part_0.top(0, n0 // 2))
    tile[0, n0 // 32 : n0 // 16] = units(part_0.low(0, n0 // 2))
    for p in ORDER:
        if p == "t":
            part_t.arrive()
            tile[1, n1 // 16 : 16] = units(part_t.total(0, 4 * cut_t))
            tile[2] = units(part_t.total(4 * cut_t, 256))
        elif p == "i":
            part_1.arrive()
            tile[1, 0 : n1 // 32] = units(part_1.top(0, n1 // 2))
            tile[1, n1 // 32 : n1 // 16] = units(part_1.low(0, n1 // 2))
        else:
            next(chains[p])

    for i, k in ((2, qp), (1, qn), (0, qd)):
        recv(f_i.at[k, pl.ds(0, 4)], own_sem[i])
        recv(f_i.at[k, pl.ds(4, 3)], own_sem[3 + i])
    for i, k in ((1, xl), (2, xr), (0, xo)):
        recv(f_t.at[k, pl.ds(0, 1)], own_sem[6 + i])
        recv(f_t.at[k, pl.ds(1, 4)], own_sem[9 + i])
    for copy in kept:
        copy.wait()
    cost_copy.wait()

    for copy in started:
        copy.wait_send()


def widen(cost, images, texts, cost_out, image_out, text_out):
    width = images.shape[-1]
    cost_out[...] = cost[...]
    for k in range(4):
        cols = pl.ds(k * width, width)
        image_out[:, cols] = images[k].reshape(-1, width).astype(F32)
        text_out[:, cols] = texts[k].reshape(-1, width).astype(F32)


def solution(mesh):
    blocks = mesh.shape["blk"]
    ring_z = mesh.shape["dp"] // 2

    def on_device(
        visual_summary_vectors, caption_summary_vectors, pairing_identifiers, valid_sample_tally,
        visual_mapping_matrix, caption_mapping_matrix, sharpness_factor, score_shift_term,
    ):
        rows, deep_i = visual_summary_vectors.shape
        deep_t, embed = caption_mapping_matrix.shape
        group, width = 4 * rows, embed // 4
        own_i, own_t = deep_i // blocks, deep_t // blocks
        vmem = pl.BlockSpec(memory_space=pltpu.VMEM)
        hbm = pl.BlockSpec(memory_space=pl.ANY)
        B = lambda *shape: pltpu.VMEM(shape, BF16)
        F = lambda *shape: pltpu.VMEM(shape, F32)
        n0, n1, nt = 4 * (own_i - 48), 4 * 48, 4 * own_t
        cost, images, texts = pl.pallas_call(
            functools.partial(kernel, blocks * rows, ring_z),
            out_shape=(
                jax.ShapeDtypeStruct((1, rows), F32),
                jax.ShapeDtypeStruct((4, own_i // 16, 16, width), BF16),
                jax.ShapeDtypeStruct((4, own_t // 16, 16, width), BF16),
            ),
            in_specs=[hbm] * 8,
            out_specs=(hbm, hbm, hbm),
            scratch_shapes=[
                pltpu.VMEM((blocks, rows), jnp.int32), pltpu.SMEM((1, blocks), jnp.int32),
                pltpu.SMEM((1,), F32), pltpu.SMEM((1,), F32), F(1, rows),
                B(deep_i, embed), B(deep_t, embed), B(4, rows, deep_i), B(4, rows, deep_t),
                B(group, embed), B(group, embed), F(group, rows), F(group, rows), F(2 * rows, embed),
                F(group, rows), F(group, rows), F(group, rows), F(group, rows), F(8, group), F(16, group),
                B(group, group), B(group, group), F(16, group), F(8, group),
                F(3, 16, group), F(3, 8, group), F(16, group),
                B(4, group, width), B(2, group // 2, width), B(6, group // 2, width),
                B(4, group, width), B(group, width), B(3, group, width),
                B(group, width), B(group, width), B(deep_i, group), B(deep_t, group),
                B(4, n0, width), B(2, n0 // 2, width), B(6, n0 // 2, width),
                B(4, n1, width), B(2, n1 // 2, width), B(6, n1 // 2, width),
                B(4, nt, width), B(nt, width), B(3, nt, width),
                F(3, 16, 16, width), B(3, ring_z - 1, 2, 16, width), B(3, ring_z - 1, 2, 16, width),
                B(3, 2, 16, width), B(3, 2, 16, width), B(3, 16, 16, width),
                pltpu.SemaphoreType.DMA((13,)),
                pltpu.SemaphoreType.DMA((128,)),
                pltpu.SemaphoreType.DMA((128,)),
            ],
            compiler_params=pltpu.CompilerParams(
                collective_id=0, has_side_effects=True, vmem_limit_bytes=60 * 1024 * 1024
            ),
            name="contrastive_step",
        )(
            pairing_identifiers.reshape(blocks, rows), valid_sample_tally, sharpness_factor, score_shift_term,
            visual_summary_vectors, caption_summary_vectors, visual_mapping_matrix, caption_mapping_matrix,
        )
        cost, grad_image, grad_text = pl.pallas_call(
            widen,
            out_shape=(
                jax.ShapeDtypeStruct((1, rows), F32),
                jax.ShapeDtypeStruct((own_i, embed), F32),
                jax.ShapeDtypeStruct((own_t, embed), F32),
            ),
            in_specs=[vmem] * 3,
            out_specs=(vmem,) * 3,
            name="widen",
        )(cost, images, texts)
        return cost.reshape(rows), grad_image, grad_text

    placed = (
        P(("dp", "blk"), None), P(("dp", "blk"), None), P("dp"), P("dp", None), P(), P(), P(), P(),
    )
    return jax.shard_map(
        on_device,
        mesh=mesh,
        in_specs=placed,
        out_specs=(P(("dp", "blk")), P("blk", None), P("blk", None)),
        check_vma=False,
    )
```

```python
import functools

import jax
import jax.numpy as jnp
from jax import lax
from jax.experimental import pallas as pl
from jax.experimental.pallas import tpu as pltpu
from jax.sharding import PartitionSpec as P

loss_scale = 256.0
epsilon = 1e-06
MESH = pl.DeviceIdType.MESH
F32 = jnp.float32
BF16 = jnp.bfloat16
ORDER = (0, "t", 2, "i", 1) + (0, 1, 2) * 5


def kernel(
    total_rows, ring_z, lab_hbm, tal_hbm, sha_hbm, shi_hbm, x_hbm, t_hbm, wv_hbm, wt_hbm,
    cost_out, f_i, f_t,
    labels, tally, sharp, shift, cost_own,
    wv, wt, xg, tg, zi, zt, inv_i, inv_t, u_scr, lab_i, row_alive, row_rad, row_cost, col_rad, txt_meta,
    slope, slope_t, stat_i, stat_t, sti_rcv, stt_rcv, stat_tot,
    gt_snd, gt_mrg, gt_rcv, gi_snd, gi_mrg, gi_rcv, d_img, d_txt, xg_t, tg_t,
    e0_snd, e0_mrg, e0_rcv, e1_snd, e1_mrg, e1_rcv, et_snd, et_mrg, et_rcv, tile, z_snd, z_rcv, y_snd, y_rcv, res,
    loc_sem, snd_sem, rcv_sem,
):
    rows = xg.shape[1]
    group = 4 * rows
    embed = zi.shape[1]
    width = embed // 4
    dp, blk = lax.axis_index("dp"), lax.axis_index("blk")
    x, q = lax.div(blk, 4), lax.rem(blk, 4)
    y, c = lax.div(q, 2), lax.rem(q, 2)
    z, yh = lax.rem(dp, ring_z), lax.div(dp, ring_z)
    xr, xl, xo = lax.rem(x + 1, 4), lax.rem(x + 3, 4), lax.rem(x + 2, 4)
    qp, qn, qd = y * 2 + 1 - c, (1 - y) * 2 + c, (1 - y) * 2 + 1 - c
    text_order = (x, xr, xl, xo)
    image_order = (q, qp, qn, qd)
    XR, XL, XO = (dp, xr * 4 + q), (dp, xl * 4 + q), (dp, xo * 4 + q)
    PT, YN, DG = (dp, x * 4 + qp), (dp, x * 4 + qn), (dp, x * 4 + qd)
    Z = {k: (yh * ring_z + lax.rem(z + k + ring_z, ring_z), blk) for k in (1, -1, 2, -2)}
    YH = ((1 - yh) * ring_z + z, blk)

    barrier = pltpu.get_barrier_semaphore()
    peers = (XR, XL, XO, PT, YN, DG, YH, *Z.values())
    for peer in peers:
        pl.semaphore_signal(barrier, inc=1, device_id=peer, device_id_type=MESH)
    loc = [
        pltpu.make_async_copy(t_hbm, tg.at[x], loc_sem.at[0]),
        pltpu.make_async_copy(x_hbm, xg.at[q], loc_sem.at[1]),
        pltpu.make_async_copy(wt_hbm, wt, loc_sem.at[2]),
        pltpu.make_async_copy(wv_hbm, wv, loc_sem.at[3]),
        pltpu.make_async_copy(lab_hbm, labels, loc_sem.at[4]),
        pltpu.make_async_copy(tal_hbm, tally, loc_sem.at[5]),
        pltpu.make_async_copy(sha_hbm, sharp, loc_sem.at[6]),
        pltpu.make_async_copy(shi_hbm, shift, loc_sem.at[7]),
    ]
    for copy in loc:
        copy.start()

    count = [0]
    started = []

    def slot():
        count[0] += 1
        return count[0] - 1

    def send(src, dst, sem, dev):
        copy = pltpu.make_async_remote_copy(
            src_ref=src, dst_ref=dst, send_sem=snd_sem.at[sem], recv_sem=rcv_sem.at[sem],
            device_id=dev, device_id_type=MESH,
        )
        copy.start()
        started.append(copy)

    def recv(dst, sem):
        pltpu.make_async_remote_copy(
            src_ref=dst, dst_ref=dst, send_sem=snd_sem.at[sem], recv_sem=rcv_sem.at[sem],
            device_id=XR, device_id_type=MESH,
        ).wait_recv()

    half = rows // 2
    halves = (pl.ds(0, half), pl.ds(half, half))

    pl.semaphore_wait(barrier, len(peers))
    loc[0].wait()
    t_sem = [slot() for _ in range(6)]
    send(tg.at[x, halves[0]], tg.at[x, halves[0]], t_sem[0], XR)
    send(tg.at[x, halves[1]], tg.at[x, halves[1]], t_sem[1], XL)
    send(tg.at[x, halves[1]], tg.at[x, halves[1]], t_sem[2], XR)
    send(tg.at[x, halves[0]], tg.at[x, halves[0]], t_sem[3], XL)
    loc[1].wait()
    x_sem = [slot() for _ in range(5)]
    for h in range(2):
        send(xg.at[q, halves[h]], xg.at[q, halves[h]], x_sem[h], YN)
    send(xg.at[q], xg.at[q], x_sem[2], PT)

    for copy in loc[4:]:
        copy.wait()
    alive_lane = lax.broadcasted_iota(jnp.int32, (8, rows), 1)
    for k in range(4):
        cols = pl.ds(k * rows, rows)
        block = 4 * text_order[k] + q
        txt_meta[0:8, cols] = jnp.broadcast_to(labels[pl.ds(block, 1), :], (8, rows)).astype(F32)
        txt_meta[8:16, cols] = jnp.where(alive_lane < tally[0, block], 1.0, 0.0)
        block = 4 * x + image_order[k]
        wide = jnp.broadcast_to(labels[pl.ds(block, 1), :].astype(F32), (rows, rows))
        lab_i[pl.ds(k * rows, rows), :] = wide.T

    def project(source, weights, unit, inverse, slots, role):
        n_rows = rows * len(slots)
        place = pl.ds(0, n_rows)

        def body(j, carry):
            cols = pl.ds(pl.multiple_of(j * 512, 512), 512)
            left = source[slots[0]] if len(slots) == 1 else jnp.concatenate([source[k] for k in slots], axis=0)
            u_scr[place, cols] = jnp.dot(left, weights[:, cols], preferred_element_type=F32)
            return carry

        lax.fori_loop(0, embed // 512, body, 0)
        u = u_scr[place, :]
        inv = 1.0 / jnp.sqrt(jnp.sum(u * u, axis=1, keepdims=True) + epsilon)
        at = pl.ds(role * rows, n_rows)
        unit[at, :] = (u * inv).astype(BF16)
        inverse[at, :] = jnp.broadcast_to(inv, (n_rows, rows))

    scale = sharp[0]
    bias = shift[0]

    def pair(first, n_rows, left, n_cols):
        at, cols = pl.ds(first, n_rows), pl.ds(left, n_cols)
        cosine = lax.dot_general(
            zi[at, :], zt[cols, :], (((1,), (1,)), ((), ())), preferred_element_type=F32
        )
        same = lab_i[at, 0:1] == txt_meta[0:1, cols]
        weight = row_alive[at, 0:1] * txt_meta[8:9, cols]
        sign = jnp.where(same, 1.0, -1.0)
        t = -sign * (scale * cosine + bias)
        e = jnp.exp(-jnp.abs(t))
        cost = (jnp.maximum(t, 0.0) + jnp.log1p(e)) * weight
        sigmoid = jnp.where(t >= 0.0, 1.0, e) / (1.0 + e)
        s = -sign * sigmoid * weight * (loss_scale / total_rows)
        s16 = s.astype(BF16)
        slope[at, cols] = s16
        s = s16.astype(F32)
        slope_t[cols, at] = s.T.astype(BF16)
        along = s * cosine * scale
        row_rad[at, :] += jnp.broadcast_to(jnp.sum(along, axis=1, keepdims=True), (n_rows, rows))
        row_cost[at, :] += jnp.broadcast_to(jnp.sum(cost, axis=1, keepdims=True), (n_rows, rows))
        col_rad[0:8, cols] += jnp.broadcast_to(jnp.sum(along, axis=0, keepdims=True), (8, n_cols))

    row_rad[...] = jnp.zeros_like(row_rad)
    row_cost[...] = jnp.zeros_like(row_cost)
    col_rad[...] = jnp.zeros_like(col_rad)
    down = lax.broadcasted_iota(jnp.int32, (rows, rows), 0)
    for k in range(4):
        row_alive[k * rows : (k + 1) * rows, :] = jnp.where(down < tally[0, 4 * x + image_order[k]], 1.0, 0.0)

    unit_sem = [slot() for _ in range(4)]

    def role_rows(role):
        return pl.ds(role * rows, rows)

    def share(role, sem):
        send(zi.at[role_rows(role)], zi.at[role_rows(role + 1)], unit_sem[sem], PT)
        send(inv_i.at[role_rows(role)], inv_i.at[role_rows(role + 1)], unit_sem[sem + 1], PT)

    def shared(role, sem):
        recv(zi.at[role_rows(role + 1)], unit_sem[sem])
        recv(inv_i.at[role_rows(role + 1)], unit_sem[sem + 1])

    loc[2].wait()
    project(tg, wt, zt, inv_t, (x,), 0)
    recv(tg.at[xl, halves[0]], t_sem[0])
    send(tg.at[xl, halves[0]], tg.at[xl, halves[0]], t_sem[4], XR)
    recv(tg.at[xr, halves[1]], t_sem[1])
    send(tg.at[xr, halves[1]], tg.at[xr, halves[1]], t_sem[5], XL)
    loc[3].wait()
    project(xg, wv, zi, inv_i, (q,), 0)
    share(0, 0)
    recv(xg.at[qn, halves[0]], x_sem[0])
    send(xg.at[qn, halves[0]], xg.at[qn, halves[0]], x_sem[3], PT)
    shared(0, 0)
    for k in range(2):
        pair(k * rows, rows, 0, rows)
    recv(tg.at[xr, halves[0]], t_sem[3])
    recv(tg.at[xl, halves[1]], t_sem[2])
    project(tg, wt, zt, inv_t, (xr, xl), 1)
    for k in range(2):
        pair(k * rows, rows, rows, 2 * rows)
    recv(xg.at[qn, halves[1]], x_sem[1])
    send(xg.at[qn, halves[1]], xg.at[qn, halves[1]], x_sem[4], PT)
    project(xg, wv, zi, inv_i, (qn,), 2)
    share(2, 2)
    recv(tg.at[xo, halves[0]], t_sem[4])
    recv(tg.at[xo, halves[1]], t_sem[5])
    project(tg, wt, zt, inv_t, (xo,), 3)
    for k in range(2):
        pair(k * rows, rows, 3 * rows, rows)
    pair(2 * rows, rows, 0, group)
    shared(2, 2)

    pair(3 * rows, rows, 0, group)

    def width_at(k):
        return pl.ds(pl.multiple_of(k * width, 128), width)

    def txt_part(k):
        part = (scale * jnp.dot(slope_t[...], zi[:, width_at(k)], preferred_element_type=F32)).astype(BF16)
        for r in range(4):
            at = pl.ds(pl.multiple_of(text_order[r] * rows, rows), rows)
            gt_snd[k, at] = part[r * rows : (r + 1) * rows]

    def img_part(k):
        part = (scale * jnp.dot(slope[...], zt[:, width_at(k)], preferred_element_type=F32)).astype(BF16)
        for r in range(4):
            at = pl.ds(pl.multiple_of(image_order[r] * rows, rows), rows)
            gi_snd[k, at] = part[r * rows : (r + 1) * rows]

    class RingSum:
        def __init__(self, snd, mrg, rcv):
            self.snd, self.mrg, self.rcv = snd, mrg, rcv
            h = snd.shape[1] // 2
            self.h, self.a, self.b = h, pl.ds(0, h), pl.ds(h, h)
            self.sems = [slot() for _ in range(6)]

        def far(self):
            send(self.snd.at[xo, self.a], self.rcv.at[0], self.sems[0], XR)
            send(self.snd.at[xo, self.b], self.rcv.at[1], self.sems[1], XL)

        def near(self):
            send(self.snd.at[xr, self.b], self.rcv.at[4], self.sems[4], XR)
            send(self.snd.at[xl, self.a], self.rcv.at[5], self.sems[5], XL)

        def merge(self):
            recv(self.rcv.at[0], self.sems[0])
            self.mrg[0] = (self.rcv[0].astype(F32) + self.snd[xr, self.a].astype(F32)).astype(BF16)
            send(self.mrg.at[0], self.rcv.at[2], self.sems[2], XR)
            recv(self.rcv.at[1], self.sems[1])
            self.mrg[1] = (self.rcv[1].astype(F32) + self.snd[xl, self.b].astype(F32)).astype(BF16)
            send(self.mrg.at[1], self.rcv.at[3], self.sems[3], XL)

        def arrive(self):
            for i in (4, 5, 2, 3):
                recv(self.rcv.at[i], self.sems[i])

        def top(self, start, size):
            at = pl.ds(start, size)
            return self.snd[x, at].astype(F32) + self.rcv[2, at].astype(F32) + self.rcv[5, at].astype(F32)

        def low(self, start, size):
            at = pl.ds(start, size)
            mine = self.snd[x, pl.ds(self.h + start, size)].astype(F32)
            return mine + self.rcv[3, at].astype(F32) + self.rcv[4, at].astype(F32)

    class PairSum:
        def __init__(self, snd, mrg, rcv):
            self.snd, self.mrg, self.rcv = snd, mrg, rcv
            self.sems = [slot() for _ in range(3)]

        def far(self):
            send(self.snd.at[qd], self.rcv.at[0], self.sems[0], PT)

        def near(self):
            send(self.snd.at[qp], self.rcv.at[1], self.sems[1], PT)

        def merge(self):
            recv(self.rcv.at[0], self.sems[0])
            self.mrg[...] = (self.rcv[0].astype(F32) + self.snd[qn].astype(F32)).astype(BF16)
            send(self.mrg, self.rcv.at[2], self.sems[2], YN)

        def arrive(self):
            recv(self.rcv.at[1], self.sems[1])
            recv(self.rcv.at[2], self.sems[2])

        def total(self, start, size):
            at = pl.ds(start, size)
            return self.snd[q, at].astype(F32) + self.rcv[1, at].astype(F32) + self.rcv[2, at].astype(F32)

    txt_sum = RingSum(gt_snd, gt_mrg, gt_rcv)
    img_sum = PairSum(gi_snd, gi_mrg, gi_rcv)
    txt_part(xo)
    txt_sum.far()
    img_part(qd)
    img_sum.far()
    row_t, cost_t = row_rad[...].T, row_cost[...].T
    for k in range(4):
        at = pl.ds(pl.multiple_of(image_order[k] * rows, rows), rows)
        stat_i[0:8, at] = row_t[0:8, k * rows : (k + 1) * rows]
        stat_i[8:16, at] = cost_t[0:8, k * rows : (k + 1) * rows]
        at = pl.ds(pl.multiple_of(text_order[k] * rows, rows), rows)
        stat_t[0:8, at] = col_rad[0:8, k * rows : (k + 1) * rows]
    st_sem = [slot() for _ in range(6)]
    for i, dev in enumerate((XR, XL, XO)):
        send(stat_t, stt_rcv.at[i], st_sem[i], dev)
    for i, dev in enumerate((PT, YN, DG)):
        send(stat_i, sti_rcv.at[i], st_sem[3 + i], dev)
    txt_part(xr)
    txt_part(xl)
    txt_sum.near()
    img_part(qn)
    img_sum.merge()
    img_part(qp)
    img_sum.near()
    img_part(q)
    txt_part(x)
    txt_sum.merge()
    recv(xg.at[qp], x_sem[2])
    recv(xg.at[qd, halves[0]], x_sem[3])
    recv(xg.at[qd, halves[1]], x_sem[4])
    for k in range(4):
        xg_t[:, k * rows : (k + 1) * rows] = xg[k].T

    for i in range(3):
        recv(sti_rcv.at[i], st_sem[3 + i])
    stat_tot[...] = stat_i[...] + sti_rcv[0] + sti_rcv[1] + sti_rcv[2]
    row_rad[...] = jnp.broadcast_to(stat_tot[0:1, :], (rows, group)).T
    cost_own[...] = stat_tot[8:9, pl.ds(pl.multiple_of(q * rows, rows), rows)] * (1.0 / total_rows)
    cost_copy = pltpu.make_async_copy(cost_own, cost_out, loc_sem.at[12])
    cost_copy.start()

    def change(out, unit, inverse, k, role, column, total):
        at = pl.ds(k * rows, rows)
        placed = pl.ds(pl.multiple_of(role * rows, rows), rows)
        u = unit[placed, width_at(column)].astype(F32)
        out[at, :] = ((total - u * row_rad[at, 0:1]) * inverse[placed, 0:1]).astype(BF16)

    def image_role(k):
        return 2 * lax.rem(k // 2 + y, 2) + lax.rem(k % 2 + c, 2)

    def text_role(k):
        ahead = lax.rem(k - x + 4, 4)
        return ahead + lax.div(ahead, 2) * (5 - 2 * ahead)

    img_sum.arrive()
    for k in range(4):
        change(d_img, zi, inv_i, k, image_role(k), q, img_sum.total(k * rows, rows))

    own_i, own_t = 16 * f_i.shape[1], 16 * f_t.shape[1]
    cut_i, cut_t = own_i - 48, own_t - 64
    part_0 = RingSum(e0_snd, e0_mrg, e0_rcv)
    part_1 = RingSum(e1_snd, e1_mrg, e1_rcv)
    deep = 4 * own_i

    def image_rows(k):
        at = pl.ds(pl.multiple_of(k * deep, 64), deep)
        part = jnp.dot(xg_t[at, :], d_img[...], preferred_element_type=F32).astype(BF16)
        for owner in range(4):
            lo, mid, hi = own_i * owner, own_i * owner + cut_i, own_i * (owner + 1)
            e0_snd[k, cut_i * owner : cut_i * (owner + 1), :] = part[lo:mid]
            e1_snd[k, 48 * owner : 48 * (owner + 1), :] = part[mid:hi]

    image_rows(xo)
    part_0.far()
    image_rows(xr)
    image_rows(xl)
    part_0.near()
    part_1.far()

    for k in range(4):
        tg_t[:, k * rows : (k + 1) * rows] = tg[k].T
    for i in range(3):
        recv(stt_rcv.at[i], st_sem[i])
    txt_total = stat_t[0:1, :] + stt_rcv[0, 0:1, :] + stt_rcv[1, 0:1, :] + stt_rcv[2, 0:1, :]
    row_rad[...] = jnp.broadcast_to(txt_total, (rows, group)).T
    txt_sum.arrive()
    for k in range(2):
        change(d_txt, zt, inv_t, k, text_role(k), x, txt_sum.top(k * rows, rows))
    for k in range(2):
        change(d_txt, zt, inv_t, 2 + k, text_role(2 + k), x, txt_sum.low(k * rows, rows))

    part_t = PairSum(et_snd, et_mrg, et_rcv)
    for k in range(4):
        part = jnp.dot(
            tg_t[4 * own_t * k : 4 * own_t * (k + 1), :], d_txt[...], preferred_element_type=F32
        ).astype(BF16)
        for owner in range(4):
            lo, mid, hi = own_t * owner, own_t * owner + cut_t, own_t * (owner + 1)
            et_snd[owner, cut_t * k : cut_t * (k + 1), :] = part[lo:mid]
            et_snd[owner, 4 * cut_t + 64 * k : 4 * cut_t + 64 * (k + 1), :] = part[mid:hi]
    part_t.far()
    part_t.near()
    part_0.merge()
    part_1.near()
    image_rows(x)
    part_t.merge()
    part_1.merge()

    own_sem = [slot() for _ in range(12)]

    def units(value):
        return value.reshape(-1, 16, width)

    def at_z(k):
        return pl.ds(2 * lax.rem(k + ring_z, ring_z), 2)

    def to_owners(p):
        plans = {
            0: ((f_i, q, 4, 0, 0, ((qd, DG), (qn, YN), (qp, PT)), 0),),
            1: (
                (f_i, q, 3, 0, 4, ((qd, DG), (qn, YN), (qp, PT)), 3),
                (f_t, x, 1, 12, 0, ((xo, XO), (xr, XR), (xl, XL)), 6),
            ),
            2: ((f_t, x, 4, 0, 1, ((xo, XO), (xr, XR), (xl, XL)), 9),),
        }[p]
        for out, mine, size, base, at, dests, sem in plans:
            for i, (k, dev) in enumerate(dests):
                send(
                    res.at[p, pl.ds(base + size * k, size)], out.at[mine, pl.ds(at, size)],
                    own_sem[sem + i], dev,
                )
            copy = pltpu.make_async_copy(
                res.at[p, pl.ds(base + size * mine, size)], out.at[mine, pl.ds(at, size)],
                loc_sem.at[8 + sem // 3],
            )
            copy.start()
            kept.append(copy)

    kept = []

    def one_of(k, unit):
        return pl.ds(2 * lax.rem(k + ring_z, ring_z) + unit, 1)

    def chain(p):
        out, got = z_snd.at[p], z_rcv.at[p]
        sems = [slot() for _ in range(8)]
        for i, k in enumerate((4, 3, -3, 1, -1)):
            out[i] = tile[p, at_z(z + k)].astype(BF16)
        send(out.at[0, pl.ds(0, 1)], got.at[0, pl.ds(0, 1)], sems[0], Z[2])
        send(out.at[0, pl.ds(1, 1)], got.at[0, pl.ds(1, 1)], sems[1], Z[-2])
        send(out.at[1], got.at[1], sems[2], Z[1])
        send(out.at[2], got.at[2], sems[3], Z[-1])
        send(out.at[3], got.at[3], sems[4], Z[1])
        send(out.at[4], got.at[4], sems[5], Z[-1])
        yield
        recv(got.at[1], sems[2])
        recv(got.at[0, pl.ds(0, 1)], sems[0])
        out[5] = (tile[p, at_z(z + 2)] + got[1].astype(F32)).astype(BF16)
        out[5, 0:1] = (tile[p, one_of(z + 2, 0)] + got[1, 0:1].astype(F32) + got[0, 0:1].astype(F32)).astype(BF16)
        send(out.at[5], got.at[5], sems[6], Z[2])
        recv(got.at[2], sems[3])
        recv(got.at[0, pl.ds(1, 1)], sems[1])
        out[6] = (tile[p, at_z(z - 2)] + got[2].astype(F32)).astype(BF16)
        out[6, 1:2] = (tile[p, one_of(z - 2, 1)] + got[2, 1:2].astype(F32) + got[0, 1:2].astype(F32)).astype(BF16)
        send(out.at[6], got.at[6], sems[7], Z[-2])
        yield
        for i in (3, 4):
            recv(got.at[i], sems[i + 1])
        value = tile[p, at_z(z)] + got[3].astype(F32) + got[4].astype(F32)
        for i in (5, 6):
            recv(got.at[i], sems[i + 1])
        y_snd[p] = (value + got[5].astype(F32) + got[6].astype(F32)).astype(BF16)
        y_sem = slot()
        send(y_snd.at[p], y_rcv.at[p], y_sem, YH)
        yield
        recv(y_rcv.at[p], y_sem)
        res[p, at_z(z)] = (y_snd[p].astype(F32) + y_rcv[p].astype(F32)).astype(BF16)
        sems = [slot() for _ in range(8)]
        mine = res.at[p, at_z(z)]
        for i, k in enumerate((2, -2, 1, -1)):
            send(mine, mine, sems[i], Z[k])
        yield
        for i, side, unit in ((0, 2, 0), (1, -2, 1)):
            near, part = res.at[p, at_z(z - side)], res.at[p, one_of(z - side, unit)]
            recv(near, sems[i])
            send(part, part, sems[4 + i], Z[side])
            send(near, near, sems[6 + i], Z[side // 2])
        yield
        for i, side, unit in ((0, 2, 0), (1, -2, 1)):
            recv(res.at[p, at_z(z - side // 2)], sems[2 + i])
            recv(res.at[p, one_of(z - 2 * side, unit)], sems[4 + i])
            recv(res.at[p, at_z(z - side - side // 2)], sems[6 + i])
        to_owners(p)
        yield

    chains = [chain(p) for p in range(3)]
    part_0.arrive()
    n0, n1 = 4 * cut_i, 4 * 48
    tile[0, 0 : n0 // 32] = units(part_0.top(0, n0 // 2))
    tile[0, n0 // 32 : n0 // 16] = units(part_0.low(0, n0 // 2))
    for p in ORDER:
        if p == "t":
            part_t.arrive()
            tile[1, n1 // 16 : 16] = units(part_t.total(0, 4 * cut_t))
            tile[2] = units(part_t.total(4 * cut_t, 256))
        elif p == "i":
            part_1.arrive()
            tile[1, 0 : n1 // 32] = units(part_1.top(0, n1 // 2))
            tile[1, n1 // 32 : n1 // 16] = units(part_1.low(0, n1 // 2))
        else:
            next(chains[p])

    for i, k in ((2, qp), (1, qn), (0, qd)):
        recv(f_i.at[k, pl.ds(0, 4)], own_sem[i])
        recv(f_i.at[k, pl.ds(4, 3)], own_sem[3 + i])
    for i, k in ((1, xl), (2, xr), (0, xo)):
        recv(f_t.at[k, pl.ds(0, 1)], own_sem[6 + i])
        recv(f_t.at[k, pl.ds(1, 4)], own_sem[9 + i])
    for copy in kept:
        copy.wait()
    cost_copy.wait()

    for copy in started:
        copy.wait_send()


def widen(cost, images, texts, cost_out, image_out, text_out):
    width = images.shape[-1]
    cost_out[...] = cost[...]
    image_out[...] = images[0].reshape(-1, width).astype(F32)
    text_out[...] = texts[0].reshape(-1, width).astype(F32)


def solution(mesh):
    blocks = mesh.shape["blk"]
    ring_z = mesh.shape["dp"] // 2

    def on_device(
        visual_summary_vectors, caption_summary_vectors, pairing_identifiers, valid_sample_tally,
        visual_mapping_matrix, caption_mapping_matrix, sharpness_factor, score_shift_term,
    ):
        rows, deep_i = visual_summary_vectors.shape
        deep_t, embed = caption_mapping_matrix.shape
        group, width = 4 * rows, embed // 4
        own_i, own_t = deep_i // blocks, deep_t // blocks
        hbm = pl.BlockSpec(memory_space=pl.ANY)
        B = lambda *shape: pltpu.VMEM(shape, BF16)
        F = lambda *shape: pltpu.VMEM(shape, F32)
        n0, n1, nt = 4 * (own_i - 48), 4 * 48, 4 * own_t
        cost, images, texts = pl.pallas_call(
            functools.partial(kernel, blocks * rows, ring_z),
            out_shape=(
                jax.ShapeDtypeStruct((1, rows), F32),
                jax.ShapeDtypeStruct((4, own_i // 16, 16, width), BF16),
                jax.ShapeDtypeStruct((4, own_t // 16, 16, width), BF16),
            ),
            in_specs=[hbm] * 8,
            out_specs=(hbm, hbm, hbm),
            scratch_shapes=[
                pltpu.VMEM((blocks, rows), jnp.int32), pltpu.SMEM((1, blocks), jnp.int32),
                pltpu.SMEM((1,), F32), pltpu.SMEM((1,), F32), F(1, rows),
                B(deep_i, embed), B(deep_t, embed), B(4, rows, deep_i), B(4, rows, deep_t),
                B(group, embed), B(group, embed), F(group, rows), F(group, rows), F(2 * rows, embed),
                F(group, rows), F(group, rows), F(group, rows), F(group, rows), F(8, group), F(16, group),
                B(group, group), B(group, group), F(16, group), F(8, group),
                F(3, 16, group), F(3, 8, group), F(16, group),
                B(4, group, width), B(2, group // 2, width), B(6, group // 2, width),
                B(4, group, width), B(group, width), B(3, group, width),
                B(group, width), B(group, width), B(deep_i, group), B(deep_t, group),
                B(4, n0, width), B(2, n0 // 2, width), B(6, n0 // 2, width),
                B(4, n1, width), B(2, n1 // 2, width), B(6, n1 // 2, width),
                B(4, nt, width), B(nt, width), B(3, nt, width),
                F(3, 16, 16, width), B(3, ring_z - 1, 2, 16, width), B(3, ring_z - 1, 2, 16, width),
                B(3, 2, 16, width), B(3, 2, 16, width), B(3, 16, 16, width),
                pltpu.SemaphoreType.DMA((13,)),
                pltpu.SemaphoreType.DMA((128,)),
                pltpu.SemaphoreType.DMA((128,)),
            ],
            compiler_params=pltpu.CompilerParams(
                collective_id=0, has_side_effects=True, vmem_limit_bytes=60 * 1024 * 1024
            ),
            name="contrastive_step",
        )(
            pairing_identifiers.reshape(blocks, rows), valid_sample_tally, sharpness_factor, score_shift_term,
            visual_summary_vectors, caption_summary_vectors, visual_mapping_matrix, caption_mapping_matrix,
        )
        cost, grad_image, grad_text = pl.pallas_call(
            widen,
            out_shape=(
                jax.ShapeDtypeStruct((1, rows), F32),
                jax.ShapeDtypeStruct((own_i, embed), F32),
                jax.ShapeDtypeStruct((own_t, embed), F32),
            ),
            grid=(4,),
            in_specs=[
                pl.BlockSpec((1, rows), lambda k: (0, 0)),
                pl.BlockSpec((1, own_i // 16, 16, width), lambda k: (k, 0, 0, 0)),
                pl.BlockSpec((1, own_t // 16, 16, width), lambda k: (k, 0, 0, 0)),
            ],
            out_specs=(
                pl.BlockSpec((1, rows), lambda k: (0, 0)),
                pl.BlockSpec((own_i, width), lambda k: (0, k)),
                pl.BlockSpec((own_t, width), lambda k: (0, k)),
            ),
            name="widen",
        )(cost, images, texts)
        return cost.reshape(rows), grad_image, grad_text

    placed = (
        P(("dp", "blk"), None), P(("dp", "blk"), None), P("dp"), P("dp", None), P(), P(), P(), P(),
    )
    return jax.shard_map(
        on_device,
        mesh=mesh,
        in_specs=placed,
        out_specs=(P(("dp", "blk")), P("blk", None), P("blk", None)),
        check_vma=False,
    )
```
